32 devices in a mesh: band: 4 (over x, core), gvec: 2 (over y), dom: 4 (over z).
Axes of the slice: x: 2, y: 2, z: 4, core: 2. Of those that a mesh axis runs over, the one named last changes fastest.
Arguments:
- coeffs: bfloat16 [16, 128, 128, 128], P(('band', 'dom'), 'gvec'), may hold values from -1.5 to 1.5
- v_local: bfloat16 [128, 128, 128], P(None, 'gvec'), may hold values from -4 to 4
- atom_pos: float32 [3, 32768], P(None, ('band', 'gvec', 'dom')), may hold values from -32 to 160
- atom_charge: float32 [32768], P(('band', 'gvec', 'dom')), may hold values from -1 to 1
- near_list: int32 [512], P(('band', 'gvec', 'dom')), may hold values from 0 to 1023, as said below
- live_count: int32 [32], P(('band', 'gvec', 'dom')), may hold values from 0 to 16, as said below
Outputs:
- waves_new: bfloat16 [16, 128, 128, 128], P(('band', 'dom'), 'gvec')
- energies: float32 [16], P(('band', 'dom'))
- resid_ratio: float32 [16], P(('band', 'dom'))
- atom_force: float32 [3, 32768], P(None, ('band', 'gvec', 'dom'))
- totals: float32 [8], replicated
The draws below stay inside these ranges and needn't reach their ends.
Inputs may be any that keep to these rules, and one draw needn't show every extreme that they name: `live_count`: the counts of all devices sum to exactly 128; some device has all 16 slots live; a device's live slots are its first ones. `near_list`: indices of the device's own atoms; the 16 entries of one device's block are distinct.
All inputs are finite; a program needn't handle non-finite values.
Results may differ from the reference program's by a relative error of at most 0.0045.
Values may be sent and summed in bfloat16 or wider, within the bound.
A program may use at most 64 MiB of HBM per device.

```python
import jax
import jax.numpy as jnp
from jax import lax

GRID = 128
CAP = 16
ATOMS_DEV = 1024
BANDS = 16
NCH = 512
LIVE = 128
NATOMS = 32768


def draw_live_count(key, part):
    owners = NCH // CAP
    key_level, key_leader, key_order = jax.random.split(key, 3)
    levels = jax.random.randint(key_level, (owners,), 0, 3)
    leader = jax.random.randint(key_leader, (), 0, owners)
    levels = jnp.where(jnp.arange(owners) == leader, 3, levels)
    shuffle = jax.random.permutation(key_order, NCH)
    scores = jnp.repeat(levels, CAP) * NCH + shuffle
    _, chosen = lax.top_k(scores, LIVE)
    counts = jnp.zeros((owners,), jnp.int32).at[chosen // CAP].add(1)
    return counts.astype(jnp.int32)


def draw_near_list(key, part):
    owners = NCH // CAP
    key_lists = jax.random.split(key, owners)

    def pick_atoms(key_one):
        return jax.random.permutation(key_one, ATOMS_DEV)[:CAP]
    lists = jax.vmap(pick_atoms)(key_lists)
    return lists.reshape(-1).astype(jnp.int32)


def block_scale(key, dims, cuts, least, high):
    level, own = 1.0, jax.random.fold_in(key, 6)
    for axis_at, shards_of in cuts:
        draws = jnp.exp(jax.random.uniform(jax.random.fold_in(own, axis_at), (shards_of,), jnp.float32, least / len(cuts), high / len(cuts)))
        level = level * jnp.repeat(draws, dims[axis_at] // shards_of).reshape([-1 if axis == axis_at else 1 for axis in range(len(dims))])
    return level


def scatter_about(key, shape, spread, most, cuts=(), kind=jnp.bfloat16):
    result = jax.random.normal(key, shape, jnp.float32) * spread
    if len(cuts) > 0:
        result = block_scale(key, shape, cuts, -0.22, 0.18) * result
    return jnp.clip(result, min=-most, max=most).astype(kind)


def setup_inputs(seed: int = 0) -> dict:
    splits = jax.random.split(jax.random.key(seed), 7)
    return {
        "coeffs": scatter_about(splits[0], (BANDS, GRID, GRID, GRID), 0.25, 1.5, ((0, 16), (1, 2))),
        "v_local": scatter_about(splits[1], (GRID, GRID, GRID), 1.0, 4.0, ((1, 2),)),
        "atom_pos": jnp.clip(-32.0 + 192.0 * jax.random.uniform(splits[2], (3, NATOMS), jnp.float32) ** block_scale(splits[2], (3, NATOMS), ((1, 32),), -0.2, 0.2), -32.0, 160.0),
        "atom_charge": jnp.clip(jax.random.uniform(splits[3], (NATOMS,), jnp.float32, -1.0, 1.0) * block_scale(splits[3], (NATOMS,), ((0, 32),), -0.4, 0.0), -1.0, 1.0),
        "near_list": draw_near_list(jax.random.fold_in(splits[6], 71), 0),
        "live_count": draw_live_count(jax.random.fold_in(splits[6], 71), 0),
    }


sigma_fractions = (1.0 / 32.0, 1.0 / 16.0, 1.0 / 8.0, 1.0 / 4.0)
kernel_weights = (1.0, 0.5, 0.25, 0.125)
force_unit = 1.0 / 4096.0
step_size = 0.5

def cosine_table(length):
    points = jnp.arange(length).astype(jnp.float32)
    angles = jnp.pi * (points[:, None] + 0.5) * points[None, :] / length
    scales = jnp.where(points == 0.0, jnp.sqrt(1.0 / length), jnp.sqrt(2.0 / length))
    return (jnp.cos(angles) * scales[None, :]).astype(jnp.bfloat16)

def occupancy(band_index, band_total):
    shifted = band_index.astype(jnp.float32) - 0.5 * band_total
    return 2.0 / (1.0 + jnp.exp(shifted / (0.125 * band_total)))

def kernels(points, centres, extent):
    values = []
    slopes = []
    for fraction in sigma_fractions:
        exponent = 0.5 / (extent * fraction) ** 2
        offset = points[:, None] - centres[None, :]
        gauss_value = jnp.exp(-exponent * offset * offset)
        values.append(gauss_value)
        slopes.append(2.0 * exponent * offset * gauss_value)
    return (jnp.concatenate(values, axis=1), jnp.concatenate(slopes, axis=1))

def charge_work(charges, density, x_start, y_start, extent, block_width):
    x_count, y_count, z_count = density.shape
    density_rows = density.reshape(x_count * y_count, z_count).astype(jnp.bfloat16)
    x_points = (x_start + jnp.arange(x_count)).astype(jnp.float32)
    y_points = (y_start + jnp.arange(y_count)).astype(jnp.float32)
    z_points = jnp.arange(z_count).astype(jnp.float32)
    weights = jnp.array(kernel_weights, jnp.float32)
    slot_total = charges.shape[1]
    blocks = charges.reshape(4, slot_total // block_width, block_width).transpose(1, 0, 2)

    def one_block(potential, block_now):
        x_value, x_slope = kernels(x_points, block_now[0], extent)
        y_value, y_slope = kernels(y_points, block_now[1], extent)
        z_value, z_slope = kernels(z_points, block_now[2], extent)
        scaled = (weights[:, None] * block_now[3][None, :]).reshape(-1)
        plane = (x_value[:, None, :] * y_value[None, :, :]).reshape(x_count * y_count, -1).astype(jnp.bfloat16)
        depth = (scaled[None, :] * z_value).astype(jnp.bfloat16)
        potential = potential + lax.dot_general(plane, depth, (((1,), (1,)), ((), ())), preferred_element_type=jnp.float32)
        tables = jnp.concatenate([z_value, z_slope], axis=1).astype(jnp.bfloat16)
        projected = jnp.dot(density_rows, tables, preferred_element_type=jnp.float32).reshape(x_count, y_count, 2, -1)
        grid_part = projected[:, :, 0, :]
        slope_part = projected[:, :, 1, :]
        along_y = lax.optimization_barrier(jnp.sum(grid_part * y_value[None], axis=1))
        slope_y = lax.optimization_barrier(jnp.sum(grid_part * y_slope[None], axis=1))
        depth_y = lax.optimization_barrier(jnp.sum(slope_part * y_value[None], axis=1))
        force_x = lax.optimization_barrier(jnp.sum(x_slope * along_y, axis=0))
        force_y = lax.optimization_barrier(jnp.sum(x_value * slope_y, axis=0))
        force_z = lax.optimization_barrier(jnp.sum(x_value * depth_y, axis=0))
        stacked = jnp.stack([force_x, force_y, force_z]) * scaled[None, :]
        forces = -force_unit * lax.optimization_barrier(jnp.sum(stacked.reshape(3, len(kernel_weights), -1), axis=1))
        return (potential, forces)
    start = jnp.zeros((x_count * y_count, z_count), jnp.float32)
    potential, forces = lax.scan(one_block, start, blocks)
    return (potential.reshape(x_count, y_count, z_count), forces.transpose(1, 0, 2).reshape(3, slot_total))

def stress_terms(weighted, x_wave, y_wave):
    over_z = lax.optimization_barrier(jnp.sum(weighted, axis=2))
    over_y = lax.optimization_barrier(jnp.sum(weighted, axis=1))
    over_x = lax.optimization_barrier(jnp.sum(weighted, axis=0))
    stress_xx = jnp.sum(x_wave * x_wave * lax.optimization_barrier(jnp.sum(over_z, axis=1)))
    stress_yy = jnp.sum(y_wave * y_wave * lax.optimization_barrier(jnp.sum(over_z, axis=0)))
    stress_zz = jnp.sum(y_wave * y_wave * lax.optimization_barrier(jnp.sum(over_y, axis=0)))
    stress_xy = jnp.sum(x_wave[:, None] * y_wave[None, :] * over_z)
    stress_xz = jnp.sum(x_wave[:, None] * y_wave[None, :] * over_y)
    stress_yz = jnp.sum(y_wave[:, None] * y_wave[None, :] * over_x)
    return jnp.stack([stress_xx, stress_yy, stress_zz, stress_xy, stress_xz, stress_yz])

def forward_band(coeff_band, cosine_wide):
    sectioned = jnp.einsum('aql,zl->aqz', coeff_band.astype(jnp.float32), cosine_wide).astype(jnp.bfloat16)
    sectioned = jnp.einsum('aqz,yq->ayz', sectioned.astype(jnp.float32), cosine_wide).astype(jnp.bfloat16)
    return jnp.einsum('ayz,xa->xyz', sectioned.astype(jnp.float32), cosine_wide).astype(jnp.bfloat16)

def backward_band(applied, cosine_wide):
    sectioned = jnp.einsum('xyz,xa->ayz', applied.astype(jnp.float32), cosine_wide).astype(jnp.bfloat16)
    sectioned = jnp.einsum('ayz,yq->aqz', sectioned.astype(jnp.float32), cosine_wide).astype(jnp.bfloat16)
    return jnp.einsum('aqz,zl->aql', sectioned.astype(jnp.float32), cosine_wide)

def reference(coeffs, v_local, atom_pos, atom_charge, near_list, live_count):
    cosines = cosine_table(GRID)
    cosine_wide = cosines.astype(jnp.float32)
    occupied = occupancy(jnp.arange(BANDS), BANDS)

    def add_band(density, inputs):
        coeff_band, weight = inputs
        real_space = forward_band(coeff_band, cosine_wide).astype(jnp.float32)
        return (density + weight * real_space * real_space, None)
    density, _ = lax.scan(add_band, jnp.zeros((GRID, GRID, GRID), jnp.float32), (coeffs, occupied))
    owners = jnp.arange(NCH) // CAP
    slot_index = jnp.arange(NCH) % CAP
    live_mask = (slot_index < live_count[owners]).astype(jnp.float32)
    atom_index = (owners * ATOMS_DEV + near_list).astype(jnp.int32)
    picked = jnp.concatenate([atom_pos[:, atom_index], (atom_charge[atom_index] * live_mask)[None, :]], axis=0)
    target = jnp.where(live_mask > 0.5, jnp.cumsum(live_mask) - 1.0, 1.0 * LIVE).astype(jnp.int32)
    charges = jnp.zeros((4, LIVE), jnp.float32).at[:, target].set(picked, mode='drop')
    potential, forces = charge_work(charges, density, 0, 0, GRID, min(256, LIVE))
    padded = forces[:, jnp.minimum(target, LIVE - 1)] * live_mask[None, :]
    atom_force = jnp.zeros((3, NATOMS), jnp.float32).at[:, atom_index].add(padded)
    embedding = jnp.sum(density * potential) / GRID ** 3
    rounded = lax.optimization_barrier(potential.astype(jnp.bfloat16))
    field_total = v_local.astype(jnp.float32) + rounded.astype(jnp.float32)
    wave_index = jnp.arange(GRID).astype(jnp.float32) * (jnp.pi / GRID)
    kinetic = 0.5 * (wave_index[:, None, None] ** 2 + wave_index[None, :, None] ** 2 + wave_index[None, None, :] ** 2)

    def update_band(weighted, inputs):
        coeff_band, weight = inputs
        real_space = forward_band(coeff_band, cosine_wide)
        applied = (field_total * real_space.astype(jnp.float32)).astype(jnp.bfloat16)
        wave_field = backward_band(applied, cosine_wide)
        coeff_wide = coeff_band.astype(jnp.float32)
        image = kinetic * coeff_wide + wave_field
        norm_sq = jnp.sum(coeff_wide * coeff_wide)
        energy = jnp.sum(coeff_wide * image) / norm_sq
        residual = image - energy * coeff_wide
        ratio_band = jnp.sum(residual * residual) / norm_sq
        updated = (coeff_wide - step_size * residual / (1.0 + kinetic)).astype(jnp.bfloat16)
        return (weighted + weight * coeff_wide * coeff_wide, (updated, energy, ratio_band))
    weighted, outputs = lax.scan(update_band, jnp.zeros((GRID, GRID, GRID), jnp.float32), (coeffs, occupied))
    waves_new, energies, resid_ratio = outputs
    stress = stress_terms(weighted, wave_index, wave_index) / GRID ** 3
    band_energy = jnp.sum(occupied * energies) / BANDS
    totals = jnp.concatenate([stress, jnp.stack([embedding, band_energy])])
    return (waves_new, energies, resid_ratio, atom_force, totals)
```

```python
import functools

import jax
import jax.numpy as jnp
import numpy as np
from jax import lax
from jax.experimental import pallas as pl
from jax.experimental.pallas import tpu as pltpu
from jax.sharding import PartitionSpec as P

sigma_fractions = (1.0 / 32.0, 1.0 / 16.0, 1.0 / 8.0, 1.0 / 4.0)
kernel_weights = (1.0, 0.5, 0.25, 0.125)
force_unit = 1.0 / 4096.0
step_size = 0.5
MESH = pl.DeviceIdType.MESH
F32 = jnp.float32
BF16 = jnp.bfloat16
HIGH = lax.Precision.HIGHEST


def cosine_table(length):
    points = np.arange(length).astype(np.float32)
    angles = np.float32(np.pi) * (points[:, None] + np.float32(0.5)) * points[None, :] / np.float32(length)
    scales = np.where(points == 0.0, np.sqrt(1.0 / length), np.sqrt(2.0 / length)).astype(np.float32)
    return (np.cos(angles.astype(np.float64)).astype(np.float32) * scales[None, :]).astype(jnp.bfloat16)


def constant_tables(length):
    cosines = cosine_table(length)
    zero = np.zeros_like(cosines)
    pair = np.stack([cosines, cosines.T])
    diagonal = np.stack(
        [np.block([[cosines.T, zero], [zero, cosines.T]]), np.block([[cosines, zero], [zero, cosines]])]
    )
    return pair, diagonal


def group_tables(sizes):
    band_size, gvec_size, dom_size = sizes
    total = band_size * gvec_size * dom_size
    at = np.arange(total)
    group = (at // (gvec_size * dom_size)) * dom_size + at % dom_size
    same = (group[:, None] == group[None, :]).astype(np.float32)
    before = (at[None, :] < at[:, None]).astype(np.float32)
    return np.stack([same, before]), group.astype(np.float32)[:, None]


def dot(left, right):
    return jnp.dot(left, right, preferred_element_type=F32)


def total_of(value):
    return jnp.sum(jnp.sum(value, axis=0, keepdims=True), axis=1, keepdims=True)


def iota(shape, axis):
    return lax.broadcasted_iota(jnp.int32, shape, axis)


def step_kernel(
    sizes, plan,
    near_ref, live_ref, pos_ref, charge_ref, cos_ref, diag_ref, group_ref, band_ref, coeff_hbm, local_hbm,
    waves_ref, force_out, misc_ref,
    coeff_ref, local_ref, stage_ref, sect_ref, held_ref, field_ref, dens_ref, going_ref, back_ref,
    image_ref, recip_ref, moment_ref, row_ref, rows_ref, tile_ref, tiles_ref, last_ref, lasts_ref,
    xg_ref, xh_ref, yg_ref, y_ref, depth_ref, zg_ref, zh_ref, scale_ref, place_ref, proj_ref,
    load_sem, local_sem, own_sem, fsend, frecv, bsend, brecv, csend, crecv,
):
    band_size, gvec_size, dom_size = sizes
    total = band_size * gvec_size * dom_size
    x_local, extent, y_share, cap, live_total, atoms = plan
    band_id, gvec_id, dom_id = lax.axis_index("band"), lax.axis_index("gvec"), lax.axis_index("dom")
    me = (band_id * gvec_size + gvec_id) * dom_size + dom_id
    band_total = band_size * dom_size
    width = len(kernel_weights) * live_total
    cells = float(extent**3)
    wave_step = np.float32(np.pi / extent)
    y_chunk = 16 if y_share % 16 == 0 else y_share
    chunks = y_share // y_chunk
    piece = 16 if x_local % 16 == 0 else x_local
    pieces = x_local // piece
    barrier = pltpu.get_barrier_semaphore()

    def peer_of(step):
        outer = step // gvec_size
        return (
            lax.rem(band_id + outer // dom_size, band_size),
            lax.rem(gvec_id + step % gvec_size, gvec_size),
            lax.rem(dom_id + outer % dom_size, dom_size),
        )

    def greet(step, carry):
        pl.semaphore_signal(barrier, inc=1, device_id=peer_of(step), device_id_type=MESH)
        return carry

    lax.fori_loop(1, total, greet, 0)

    def load_of(part):
        window = pl.ds(part * piece, piece)
        return pltpu.make_async_copy(coeff_hbm.at[0, window], coeff_ref.at[window], load_sem.at[part])

    for part in range(pieces):
        load_of(part).start()
    local_copy = pltpu.make_async_copy(local_hbm, local_ref, local_sem)
    local_copy.start()

    def broadcast(kind, src, dst):
        def copy_of(step):
            return pltpu.make_async_remote_copy(
                src_ref=src, dst_ref=dst.at[me],
                send_sem=csend.at[kind, step], recv_sem=crecv.at[kind, step],
                device_id=peer_of(step), device_id_type=MESH,
            )

        def send(step, carry):
            copy_of(step).start()
            return carry

        def finish(step, carry):
            copy_of(step).wait()
            return carry

        def start():
            lax.fori_loop(1, total, send, 0)

        def wait(first, stop):
            lax.fori_loop(first, stop, finish, 0)

        return start, wait

    lanes = row_ref.shape[1]
    lane = iota((1, lanes), 1)
    near_row = jnp.full((1, lanes), -1, jnp.int32)
    for quantity in range(4):
        for slot in range(cap):
            near_row = jnp.where(lane == quantity * cap + slot, near_ref[slot], near_row)
    live = live_ref[0]
    chosen = (iota((atoms, lanes), 0) == near_row).astype(F32)
    picked_pos = jnp.dot(pos_ref[...], chosen, precision=HIGH, preferred_element_type=F32)
    picked_charge = jnp.dot(charge_ref[...], chosen, precision=HIGH, preferred_element_type=F32)
    row = jnp.zeros((1, lanes), F32)
    for quantity in range(3):
        part = (lane >= quantity * cap) & (lane < (quantity + 1) * cap)
        row = jnp.where(part, picked_pos[quantity : quantity + 1], row)
    part = (lane >= 3 * cap) & (lane < 3 * cap + live) & (lane < 4 * cap)
    row = jnp.where(part, picked_charge, row)
    row = jnp.where(lane == 4 * cap, live.astype(F32), row)
    row_ref[...] = row
    rows_ref[me] = row

    group = piece

    def forward(index, carry):
        load_of(index).wait()
        for pair in range(group // 2):
            first = index * group + 2 * pair
            both = jnp.concatenate([coeff_ref[first], coeff_ref[first + 1]], axis=1)
            section = dot(both, diag_ref[0]).astype(BF16)
            result = dot(cos_ref[0], section)
            stage_ref[pl.ds(2 * pair * extent, extent)] = result[:, :extent]
            stage_ref[pl.ds((2 * pair + 1) * extent, extent)] = result[:, extent:]
        window = pl.ds(pl.multiple_of(index * group, group), group)

        def spread(outer, inner_carry):
            for inner in range(8):
                y = outer * 8 + inner
                sect_ref[y, window] = stage_ref[pl.ds(y, group, stride=extent)].astype(BF16)
            return inner_carry

        lax.fori_loop(0, extent // 8, spread, 0)
        return carry

    lax.fori_loop(0, pieces, forward, 0)
    pl.semaphore_wait(barrier, total - 1)

    start_rows, wait_rows = broadcast(0, row_ref, rows_ref)
    start_rows()

    def gvec_peer(step):
        return (band_id, lax.rem(gvec_id + step, gvec_size), dom_id)

    def forward_copy(step, chunk):
        owner = lax.rem(gvec_id + step, gvec_size)
        return pltpu.make_async_remote_copy(
            src_ref=sect_ref.at[pl.ds(owner * y_share + chunk * y_chunk, y_chunk)],
            dst_ref=held_ref.at[gvec_id, pl.ds(chunk * y_chunk, y_chunk)],
            send_sem=fsend.at[step, chunk], recv_sem=frecv.at[step, chunk],
            device_id=gvec_peer(step), device_id_type=MESH,
        )

    for chunk in range(chunks):
        for step in range(1, gvec_size):
            forward_copy(step, chunk).start()
    own_copy = pltpu.make_async_copy(
        sect_ref.at[pl.ds(gvec_id * y_share, y_share)], held_ref.at[gvec_id], own_sem.at[0]
    )
    own_copy.start()

    local_copy.wait()
    x_block = 16

    def turn_local(index, carry):
        window = pl.ds(pl.multiple_of(index * x_block, x_block), x_block)
        stage_ref[pl.ds(0, x_block * y_share)] = (
            local_ref[window].astype(F32).reshape(x_block * y_share, extent)
        )

        def turn(outer, inner_carry):
            for inner in range(8):
                y = outer * 8 + inner
                field_ref[y, window] = stage_ref[pl.ds(y, x_block, stride=y_share)]
            return inner_carry

        lax.fori_loop(0, y_share // 8, turn, 0)
        return carry

    lax.fori_loop(0, extent // x_block, turn_local, 0)

    wait_rows(1, total)
    rows = rows_ref[:, 0, :]
    count = rows[:, 4 * cap : 4 * cap + 1]
    count_wide = jnp.broadcast_to(count, (total, live_total))
    offset = jnp.dot(group_ref[1], count_wide, precision=HIGH, preferred_element_type=F32)
    order = iota((total, live_total), 1).astype(F32)
    holds = ((order >= offset) & (order < offset + count_wide)).astype(F32)
    slot_at = jnp.sum(holds * (order - offset), axis=0, keepdims=True)
    spread_rows = lax.dot_general(
        rows, holds, (((0,), (0,)), ((), ())), precision=HIGH, preferred_element_type=F32
    )
    here = (iota((cap, live_total), 0).astype(F32) == slot_at).astype(F32)
    centre = [
        jnp.sum(spread_rows[k * cap : (k + 1) * cap] * here, axis=0, keepdims=True) for k in range(4)
    ]
    mine = (iota((total, 1), 0) == me).astype(F32)
    own_offset = jnp.sum(mine * offset[:, :1], axis=0, keepdims=True)
    place_ref[...] = jnp.broadcast_to(own_offset, place_ref.shape)

    x_points = iota((extent, live_total), 0).astype(F32)
    y_points = (iota((y_share, live_total), 0) + gvec_id * y_share).astype(F32)
    for k, fraction in enumerate(sigma_fractions):
        exponent = 0.5 / (extent * fraction) ** 2
        window = slice(k * live_total, (k + 1) * live_total)
        scaled = kernel_weights[k] * centre[3]
        scale_ref[:, window] = scaled
        away = x_points - centre[0]
        value = jnp.exp(-exponent * away * away)
        xg_ref[:, window] = value
        xh_ref[:, window] = 2.0 * exponent * away * value
        away = y_points - centre[1]
        value = jnp.exp(-exponent * away * away)
        slope = 2.0 * exponent * away * value
        yg_ref[:, window] = value
        for part in range(live_total // 128):
            y_ref[0, k * live_total // 128 + part] = value[:, part * 128 : (part + 1) * 128]
            y_ref[1, k * live_total // 128 + part] = slope[:, part * 128 : (part + 1) * 128]
        away = x_points - centre[2]
        value = jnp.exp(-exponent * away * away)
        depth_ref[:, window] = (scaled * value).astype(BF16)
        zg_ref[:, window] = value.astype(BF16)
        zh_ref[:, window] = (2.0 * exponent * away * value).astype(BF16)

    block = min(width, 512)

    def add_field(y, carry):
        value = None
        for part in range(width // block):
            window = slice(part * block, (part + 1) * block)
            plane = (xg_ref[:, window] * yg_ref[pl.ds(y, 1), window]).astype(BF16)
            term = lax.dot_general(
                plane, depth_ref[:, window], (((1,), (1,)), ((), ())), preferred_element_type=F32
            )
            value = term if value is None else value + term
        field_ref[y] += value.astype(BF16).astype(F32)
        return carry

    lax.fori_loop(0, y_share, add_field, 0)

    def back_copy(step, chunk, part):
        owner = lax.rem(gvec_id + step, gvec_size)
        return pltpu.make_async_remote_copy(
            src_ref=going_ref.at[chunk, pl.ds(owner * x_local + part * piece, piece)],
            dst_ref=back_ref.at[gvec_id, chunk, pl.ds(part * piece, piece)],
            send_sem=bsend.at[step, chunk, part], recv_sem=brecv.at[step, chunk, part],
            device_id=gvec_peer(step), device_id_type=MESH,
        )

    def own_back(chunk):
        return pltpu.make_async_copy(
            going_ref.at[chunk, pl.ds(gvec_id * x_local, x_local)],
            back_ref.at[gvec_id, chunk], own_sem.at[1 + chunk],
        )

    own_copy.wait()

    def middle(chunk, carry):
        for step in range(1, gvec_size):
            forward_copy(step, chunk).wait_recv()
        for pair in range(y_chunk // 2):
            first = chunk * y_chunk + 2 * pair
            both = jnp.concatenate(
                [
                    jnp.concatenate([held_ref[source, first + side] for source in range(gvec_size)], axis=0)
                    for side in range(2)
                ],
                axis=1,
            )
            wide = dot(cos_ref[0], both).astype(BF16).astype(F32)
            square = (wide * wide).astype(BF16)
            dens_ref[first] = square[:, :extent]
            dens_ref[first + 1] = square[:, extent:]
            fields = jnp.concatenate([field_ref[first], field_ref[first + 1]], axis=1)
            result = dot(cos_ref[1], (fields * wide).astype(BF16))
            stage_ref[pl.ds(2 * pair * extent, extent)] = result[:, :extent]
            stage_ref[pl.ds((2 * pair + 1) * extent, extent)] = result[:, extent:]

        def spread(outer, inner_carry):
            for inner in range(8):
                a = outer * 8 + inner
                going_ref[chunk, a] = stage_ref[pl.ds(a, y_chunk, stride=extent)].astype(BF16)
            return inner_carry

        lax.fori_loop(0, extent // 8, spread, 0)
        for part in range(pieces):
            for step in range(1, gvec_size):
                back_copy(step, chunk, part).start()
        own_back(chunk).start()
        return carry

    lax.fori_loop(0, chunks, middle, 0)

    q_wave = iota((extent, extent), 0).astype(F32) * wave_step
    l_wave = iota((extent, extent), 1).astype(F32) * wave_step
    plane_kinetic = 0.5 * (q_wave * q_wave + l_wave * l_wave)
    moment_ref[...] = jnp.zeros_like(moment_ref)

    def x_wave_of(a):
        return jnp.full((1, 1), gvec_id * x_local + a, jnp.int32).astype(F32) * wave_step

    def coefficients(index, carry):
        zero, one, two = 0.0, 0.0, 0.0
        for inner in range(4):
            a = index * 4 + inner
            wide = coeff_ref[a].astype(F32)
            x_wave = x_wave_of(a)
            square = wide * wide
            by_x = square * x_wave
            zero, one, two = zero + square, one + by_x, two + by_x * x_wave
            recip_ref[a] = step_size / (1.0 + 0.5 * x_wave * x_wave + plane_kinetic)
        moment_ref[0] += zero
        moment_ref[1] += one
        moment_ref[2] += two
        return carry

    lax.fori_loop(0, x_local // 4, coefficients, 0)
    group_id = band_id * dom_size + dom_id
    shifted = jnp.full((1, 1), group_id, jnp.int32).astype(F32) - 0.5 * band_total
    weight = 2.0 / (1.0 + jnp.exp(shifted / (0.125 * band_total)))
    terms = (
        moment_ref[2],
        moment_ref[0] * q_wave * q_wave,
        moment_ref[0] * l_wave * l_wave,
        moment_ref[1] * q_wave,
        moment_ref[1] * l_wave,
        moment_ref[0] * q_wave * l_wave,
    )
    stress = [weight * total_of(term) / cells for term in terms]

    y_block = 16 if y_share % 16 == 0 else y_share
    x_part = 32

    def project(index, carry):
        at = pl.ds(pl.multiple_of(index * 128, 128), 128)
        tables = jnp.concatenate([zg_ref[:, at], zh_ref[:, at]], axis=1)
        sums = [jnp.zeros((1, 128), F32) for _ in range(4)]
        for x_at in range(extent // x_part):
            x_window = pl.ds(x_at * x_part, x_part)

            def over_y(outer, accs):
                along, slope, deep = accs
                left = dens_ref[pl.ds(outer * y_block, y_block), x_window].reshape(y_block * x_part, extent)
                result = dot(left, tables)
                for inner in range(y_block):
                    y = outer * y_block + inner
                    rows_at = slice(inner * x_part, (inner + 1) * x_part)
                    value, derivative = y_ref[0, index, pl.ds(y, 1)], y_ref[1, index, pl.ds(y, 1)]
                    along = along + result[rows_at, :128] * value
                    slope = slope + result[rows_at, :128] * derivative
                    deep = deep + result[rows_at, 128:] * value
                return along, slope, deep

            start = tuple(jnp.zeros((x_part, 128), F32) for _ in range(3))
            along, slope, deep = lax.fori_loop(0, y_share // y_block, over_y, start)
            value, derivative = xg_ref[x_window, at], xh_ref[x_window, at]
            for at_sum, term in enumerate((derivative * along, value * slope, value * deep, value * along)):
                sums[at_sum] = sums[at_sum] + jnp.sum(term, axis=0, keepdims=True)
        for at_sum in range(4):
            proj_ref[at_sum : at_sum + 1, at] = sums[at_sum] * scale_ref[:, at]
        return carry

    lax.fori_loop(0, width // 128, project, 0)
    folded = jnp.zeros((4, live_total), F32)
    for k in range(len(kernel_weights)):
        folded = folded + proj_ref[:, k * live_total : (k + 1) * live_total]
    tile_ref[0:3] = (-force_unit * weight) * folded[0:3]
    embedding = weight * jnp.sum(folded[3:4], axis=1, keepdims=True) / cells
    line = jnp.zeros((1, live_total), F32)
    tile_lane = iota((1, live_total), 1)
    for at, value in enumerate(stress + [embedding]):
        line = jnp.where(tile_lane == at, value, line)
    tile_ref[3:4] = line
    tiles_ref[me] = tile_ref[...]
    start_tiles, wait_tiles = broadcast(1, tile_ref, tiles_ref)
    start_tiles()

    for chunk in range(chunks):
        own_back(chunk).wait()
    norms, inners, squares = [], [], []
    for part in range(pieces):
        for chunk in range(chunks):
            for step in range(1, gvec_size):
                back_copy(step, chunk, part).wait_recv()

        def image_of(index, carry):
            norm, inner = carry
            for pair in range(2):
                first = part * piece + 4 * index + 2 * pair
                both = jnp.concatenate(
                    [
                        jnp.concatenate(
                            [
                                back_ref[source, chunk, first + side]
                                for source in range(gvec_size)
                                for chunk in range(chunks)
                            ],
                            axis=0,
                        )
                        for side in range(2)
                    ],
                    axis=1,
                )
                section = dot(cos_ref[1], both).astype(BF16)
                waves = dot(section, diag_ref[1])
                for side in range(2):
                    a = first + side
                    wide = coeff_ref[a].astype(F32)
                    x_wave = x_wave_of(a)
                    image = (0.5 * x_wave * x_wave + plane_kinetic) * wide
                    image = image + waves[:, side * extent : (side + 1) * extent]
                    image_ref[a] = image
                    norm = norm + jnp.sum((wide * wide).reshape(-1, 8, extent), axis=0)
                    inner = inner + jnp.sum((wide * image).reshape(-1, 8, extent), axis=0)
            return norm, inner

        empty = jnp.zeros((8, extent), F32)
        norm, inner = lax.fori_loop(0, piece // 4, image_of, (empty, empty))
        norm, inner = total_of(norm), total_of(inner)
        filled = norm > 0.0
        energy = jnp.where(filled, inner / jnp.where(filled, norm, 1.0), 0.0)

        def residual_of(index, square):
            for side in range(4):
                a = part * piece + 4 * index + side
                wide = coeff_ref[a].astype(F32)
                image = image_ref[a]
                residual = image - energy * wide
                square = square + jnp.sum((residual * residual).reshape(-1, 8, extent), axis=0)
                image_ref[a] = wide - image * recip_ref[a]
            return square

        square = total_of(lax.fori_loop(0, piece // 4, residual_of, empty))
        norms.append(norm)
        inners.append(inner)
        squares.append(square)

    def merged(parts):
        norm = sum(part[0] for part in parts)
        inner = sum(part[1] for part in parts)
        filled = norm > 0.0
        energy = jnp.where(filled, inner / jnp.where(filled, norm, 1.0), 0.0)
        square = 0.0
        for part_norm, part_inner, part_square in parts:
            filled = part_norm > 0.0
            part_energy = jnp.where(filled, part_inner / jnp.where(filled, part_norm, 1.0), 0.0)
            away = part_energy - energy
            square = square + part_square + away * away * part_norm
        return norm, inner, square

    own = merged(list(zip(norms, inners, squares)))
    last_lane = iota(last_ref.shape, 1)
    last = jnp.zeros(last_ref.shape, F32)
    for at, value in enumerate(own):
        last = jnp.where(last_lane == at, value, last)
    last_ref[...] = last
    lasts_ref[me] = last
    start_last, wait_last = broadcast(2, last_ref, lasts_ref)
    start_last()
    wait_last(1, gvec_size)
    parts = []
    for source in range(gvec_size):
        other = lasts_ref[(band_id * gvec_size + source) * dom_size + dom_id]
        parts.append(tuple(other[:, at : at + 1] for at in range(3)))
    norm, inner, square = merged(parts)
    energy = inner / norm

    def update(index, carry):
        for side in range(4):
            a = index * 4 + side
            wide = coeff_ref[a].astype(F32)
            waves_ref[0, a] = (image_ref[a] + energy * (wide * recip_ref[a])).astype(BF16)
        return carry

    lax.fori_loop(0, x_local // 4, update, 0)

    wait_tiles(1, total)
    summed = tiles_ref[0]
    for source in range(1, total):
        summed = summed + tiles_ref[source]
    slot_lanes = (iota((live_total, 128), 0).astype(F32) - place_ref[0:1, 0:1]) == iota(
        (live_total, 128), 1
    ).astype(F32)
    slot_lanes = slot_lanes & (iota((live_total, 128), 1) < live)
    slot_force = jnp.dot(summed, slot_lanes.astype(F32), precision=HIGH, preferred_element_type=F32)
    near_column = jnp.full((128, 1), -1, jnp.int32)
    for slot in range(cap):
        near_column = jnp.where(iota((128, 1), 0) == slot, near_ref[slot], near_column)
    at_atom = (iota((128, atoms), 1) == near_column).astype(F32)
    atom_force = jnp.dot(slot_force, at_atom, precision=HIGH, preferred_element_type=F32)
    force_out[...] = atom_force[0:3]

    wait_last(gvec_size, total)
    lasts = lasts_ref[:, 0, :]
    both = jnp.dot(group_ref[0], lasts, precision=HIGH, preferred_element_type=F32)
    band_energy = both[:, 1:2] / both[:, 0:1]
    occupied = 2.0 / (1.0 + jnp.exp((band_ref[...] - 0.5 * band_total) / (0.125 * band_total)))
    band_sum = jnp.sum(occupied * band_energy, axis=0, keepdims=True) / float(gvec_size * band_total)
    misc_lane = iota((1, 128), 1)
    misc_ref[0:1] = jnp.broadcast_to(energy, (1, 128))
    misc_ref[1:2] = jnp.broadcast_to(square / norm, (1, 128))
    misc_ref[2:3] = jnp.where(misc_lane == 7, band_sum, summed[3:4, :128])
    misc_ref[3:8] = jnp.zeros((5, 128), F32)

    for step in range(1, gvec_size):
        for chunk in range(chunks):
            forward_copy(step, chunk).wait_send()
            for part in range(pieces):
                back_copy(step, chunk, part).wait_send()


def per_device(sizes, coeffs, v_local, atom_pos, atom_charge, near_list, live_count):
    gvec_size = sizes[1]
    total = sizes[0] * sizes[1] * sizes[2]
    local_bands, x_local, extent, _ = coeffs.shape
    assert local_bands == 1
    y_share = v_local.shape[1]
    cap = near_list.shape[0]
    atoms = atom_pos.shape[1]
    live_total = total * cap // 4
    width = len(kernel_weights) * live_total
    y_chunk = 16 if y_share % 16 == 0 else y_share
    chunks = y_share // y_chunk
    piece = 16 if x_local % 16 == 0 else x_local
    pieces = x_local // piece
    lanes = -(-(4 * cap + 1) // 128) * 128
    pair, diagonal = constant_tables(extent)
    groups, bands = group_tables(sizes)
    vmem = pl.BlockSpec(memory_space=pltpu.VMEM)
    smem = pl.BlockSpec(memory_space=pltpu.SMEM)
    hbm = pl.BlockSpec(memory_space=pl.ANY)
    plan = (x_local, extent, y_share, cap, live_total, atoms)
    deep = max(piece, y_chunk, 16)
    dma = pltpu.SemaphoreType.DMA
    waves_new, atom_force, misc = pl.pallas_call(
        functools.partial(step_kernel, sizes, plan),
        out_shape=(
            jax.ShapeDtypeStruct(coeffs.shape, BF16),
            jax.ShapeDtypeStruct((3, atoms), F32),
            jax.ShapeDtypeStruct((8, 128), F32),
        ),
        in_specs=[smem, smem, vmem, vmem, vmem, vmem, vmem, vmem, hbm, hbm],
        out_specs=(vmem, vmem, vmem),
        scratch_shapes=[
            pltpu.VMEM((x_local, extent, extent), BF16),
            pltpu.VMEM(v_local.shape, BF16),
            pltpu.VMEM((deep * extent, extent), F32),
            pltpu.VMEM((extent, x_local, extent), BF16),
            pltpu.VMEM((gvec_size, y_share, x_local, extent), BF16),
            pltpu.VMEM((y_share, extent, extent), F32),
            pltpu.VMEM((y_share, extent, extent), BF16),
            pltpu.VMEM((chunks, extent, y_chunk, extent), BF16),
            pltpu.VMEM((gvec_size, chunks, x_local, y_chunk, extent), BF16),
            pltpu.VMEM((x_local, extent, extent), F32),
            pltpu.VMEM((x_local, extent, extent), F32),
            pltpu.VMEM((3, extent, extent), F32),
            pltpu.VMEM((1, lanes), F32),
            pltpu.VMEM((total, 1, lanes), F32),
            pltpu.VMEM((4, live_total), F32),
            pltpu.VMEM((total, 4, live_total), F32),
            pltpu.VMEM((1, 128), F32),
            pltpu.VMEM((total, 1, 128), F32),
            pltpu.VMEM((extent, width), F32),
            pltpu.VMEM((extent, width), F32),
            pltpu.VMEM((y_share, width), F32),
            pltpu.VMEM((2, width // 128, y_share, 128), F32),
            pltpu.VMEM((extent, width), BF16),
            pltpu.VMEM((extent, width), BF16),
            pltpu.VMEM((extent, width), BF16),
            pltpu.VMEM((1, width), F32),
            pltpu.VMEM((8, 128), F32),
            pltpu.VMEM((4, width), F32),
            dma((pieces,)),
            dma,
            dma((1 + chunks,)),
            dma((gvec_size, chunks)),
            dma((gvec_size, chunks)),
            dma((gvec_size, chunks, pieces)),
            dma((gvec_size, chunks, pieces)),
            dma((3, total)),
            dma((3, total)),
        ],
        compiler_params=pltpu.CompilerParams(
            collective_id=0, has_side_effects=True, vmem_limit_bytes=58 * 1024 * 1024
        ),
        name="step",
    )(
        near_list, live_count, atom_pos, atom_charge.reshape(1, atoms), jnp.asarray(pair),
        jnp.asarray(diagonal), jnp.asarray(groups), jnp.asarray(bands), coeffs, v_local,
    )
    return (waves_new, misc[0, :1], misc[1, :1], atom_force, misc[2, :8])


def solution(mesh):
    sizes = (mesh.shape["band"], mesh.shape["gvec"], mesh.shape["dom"])
    return jax.shard_map(
        functools.partial(per_device, sizes),
        mesh=mesh,
        in_specs=(
            P(("band", "dom"), "gvec", None, None),
            P(None, "gvec", None),
            P(None, ("band", "gvec", "dom")),
            P(("band", "gvec", "dom")),
            P(("band", "gvec", "dom")),
            P(("band", "gvec", "dom")),
        ),
        out_specs=(
            P(("band", "dom"), "gvec", None, None),
            P(("band", "dom")),
            P(("band", "dom")),
            P(None, ("band", "gvec", "dom")),
            P(),
        ),
        check_vma=False,
    )
```

```python
import functools

import jax
import jax.numpy as jnp
import numpy as np
from jax import lax
from jax.experimental import pallas as pl
from jax.experimental.pallas import tpu as pltpu
from jax.sharding import PartitionSpec as P

sigma_fractions = (1.0 / 32.0, 1.0 / 16.0, 1.0 / 8.0, 1.0 / 4.0)
kernel_weights = (1.0, 0.5, 0.25, 0.125)
force_unit = 1.0 / 4096.0
step_size = 0.5
MESH = pl.DeviceIdType.MESH
F32 = jnp.float32
BF16 = jnp.bfloat16
HIGH = lax.Precision.HIGHEST


def cosine_table(length):
    points = np.arange(length).astype(np.float32)
    angles = np.float32(np.pi) * (points[:, None] + np.float32(0.5)) * points[None, :] / np.float32(length)
    scales = np.where(points == 0.0, np.sqrt(1.0 / length), np.sqrt(2.0 / length)).astype(np.float32)
    return (np.cos(angles.astype(np.float64)).astype(np.float32) * scales[None, :]).astype(jnp.bfloat16)


def constant_tables(length):
    cosines = cosine_table(length)
    zero = np.zeros_like(cosines)
    pair = np.stack([cosines, cosines.T])
    diagonal = np.stack(
        [np.block([[cosines.T, zero], [zero, cosines.T]]), np.block([[cosines, zero], [zero, cosines]])]
    )
    return pair, diagonal


def group_tables(sizes):
    band_size, gvec_size, dom_size = sizes
    total = band_size * gvec_size * dom_size
    at = np.arange(total)
    group = (at // (gvec_size * dom_size)) * dom_size + at % dom_size
    same = (group[:, None] == group[None, :]).astype(np.float32)
    before = (at[None, :] < at[:, None]).astype(np.float32)
    return np.stack([same, before]), group.astype(np.float32)[:, None]


def dot(left, right):
    return jnp.dot(left, right, preferred_element_type=F32)


def total_of(value):
    return jnp.sum(jnp.sum(value, axis=0, keepdims=True), axis=1, keepdims=True)


def iota(shape, axis):
    return lax.broadcasted_iota(jnp.int32, shape, axis)


def step_kernel(
    sizes, plan,
    near_hbm, live_ref, pos_hbm, charge_hbm, cos_hbm, diag_hbm, group_hbm, band_hbm, coeff_hbm, local_hbm,
    waves_ref, force_out, misc_ref,
    near_ref, pos_ref, charge_ref, cos_ref, diag_ref, group_ref, band_ref, coeff_ref, local_ref, stage_ref, sect_ref, held_ref, field_ref, dens_ref, going_ref, back_ref,
    image_ref, recip_ref, moment_ref, row_ref, rows_ref, tile_ref, tiles_ref, last_ref, lasts_ref,
    xg_ref, xh_ref, yg_ref, y_ref, depth_ref, zg_ref, zh_ref, scale_ref, place_ref, proj_ref,
    load_sem, local_sem, small_sem, own_sem, fsend, frecv, bsend, brecv, csend, crecv,
):
    band_size, gvec_size, dom_size = sizes
    total = band_size * gvec_size * dom_size
    x_local, extent, y_share, cap, live_total, atoms = plan
    band_id, gvec_id, dom_id = lax.axis_index("band"), lax.axis_index("gvec"), lax.axis_index("dom")
    me = (band_id * gvec_size + gvec_id) * dom_size + dom_id
    band_total = band_size * dom_size
    width = len(kernel_weights) * live_total
    cells = float(extent**3)
    wave_step = np.float32(np.pi / extent)
    y_chunk = 16 if y_share % 16 == 0 else y_share
    chunks = y_share // y_chunk
    piece = 16 if x_local % 16 == 0 else x_local
    pieces = x_local // piece
    barrier = pltpu.get_barrier_semaphore()

    def load_of(part):
        window = pl.ds(part * piece, piece)
        return pltpu.make_async_copy(coeff_hbm.at[0, window], coeff_ref.at[window], load_sem.at[part])

    smalls = [
        pltpu.make_async_copy(source, target, small_sem.at[at])
        for at, (source, target) in enumerate(
            (
                (near_hbm, near_ref), (pos_hbm, pos_ref), (charge_hbm, charge_ref),
                (cos_hbm, cos_ref), (diag_hbm, diag_ref), (group_hbm, group_ref), (band_hbm, band_ref),
            )
        )
    ]
    for copy in smalls:
        copy.start()
    for part in range(pieces):
        load_of(part).start()
    local_copy = pltpu.make_async_copy(local_hbm, local_ref, local_sem)
    local_copy.start()

    band_at = [lax.rem(band_id + shift, band_size) for shift in range(band_size)]
    gvec_at = [lax.rem(gvec_id + shift, gvec_size) for shift in range(gvec_size)]
    dom_at = [lax.rem(dom_id + shift, dom_size) for shift in range(dom_size)]

    def peer_of(step):
        outer = step // gvec_size
        return band_at[outer // dom_size], gvec_at[step % gvec_size], dom_at[outer % dom_size]

    for step in range(1, total):
        pl.semaphore_signal(barrier, inc=1, device_id=peer_of(step), device_id_type=MESH)

    def broadcast(kind, src, dst):
        def copy_of(step):
            return pltpu.make_async_remote_copy(
                src_ref=src, dst_ref=dst.at[me],
                send_sem=csend.at[kind, step], recv_sem=crecv.at[kind, step],
                device_id=peer_of(step), device_id_type=MESH,
            )

        def start():
            for step in range(1, total):
                copy_of(step).start()

        def wait(first, stop):
            for step in range(first, stop):
                copy_of(step).wait()

        return start, wait

    for copy in smalls:
        copy.wait()

    lanes = row_ref.shape[1]
    lane = iota((1, lanes), 1)
    near_row = jnp.full((1, lanes), -1, jnp.int32)
    for quantity in range(4):
        for slot in range(cap):
            near_row = jnp.where(lane == quantity * cap + slot, near_ref[slot], near_row)
    live = live_ref[0]
    chosen = (iota((atoms, lanes), 0) == near_row).astype(F32)
    picked_pos = jnp.dot(pos_ref[...], chosen, precision=HIGH, preferred_element_type=F32)
    picked_charge = jnp.dot(charge_ref[...], chosen, precision=HIGH, preferred_element_type=F32)
    row = jnp.zeros((1, lanes), F32)
    for quantity in range(3):
        part = (lane >= quantity * cap) & (lane < (quantity + 1) * cap)
        row = jnp.where(part, picked_pos[quantity : quantity + 1], row)
    part = (lane >= 3 * cap) & (lane < 3 * cap + live) & (lane < 4 * cap)
    row = jnp.where(part, picked_charge, row)
    row = jnp.where(lane == 4 * cap, live.astype(F32), row)
    row_ref[...] = row
    rows_ref[me] = row

    group = piece

    def forward(index, carry):
        load_of(index).wait()
        for pair in range(group // 2):
            first = index * group + 2 * pair
            both = jnp.concatenate([coeff_ref[first], coeff_ref[first + 1]], axis=1)
            section = dot(both, diag_ref[0]).astype(BF16)
            result = dot(cos_ref[0], section)
            stage_ref[pl.ds(2 * pair * extent, extent)] = result[:, :extent]
            stage_ref[pl.ds((2 * pair + 1) * extent, extent)] = result[:, extent:]
        window = pl.ds(pl.multiple_of(index * group, group), group)

        def spread(outer, inner_carry):
            for inner in range(8):
                y = outer * 8 + inner
                sect_ref[y, window] = stage_ref[pl.ds(y, group, stride=extent)].astype(BF16)
            return inner_carry

        lax.fori_loop(0, extent // 8, spread, 0)
        return carry

    ahead = pieces // 2

    def gvec_peer(step):
        return (band_id, gvec_at[step], dom_id)

    def lead_copy(step):
        owner = gvec_at[step]
        window = pl.ds(0, ahead * piece)
        return pltpu.make_async_remote_copy(
            src_ref=sect_ref.at[pl.ds(owner * y_share, y_share), window],
            dst_ref=held_ref.at[gvec_id, :, window],
            send_sem=fsend.at[step, chunks], recv_sem=frecv.at[step, chunks],
            device_id=gvec_peer(step), device_id_type=MESH,
        )

    def forward_copy(step, chunk):
        owner = gvec_at[step]
        window = pl.ds(ahead * piece, x_local - ahead * piece)
        return pltpu.make_async_remote_copy(
            src_ref=sect_ref.at[pl.ds(owner * y_share + chunk * y_chunk, y_chunk), window],
            dst_ref=held_ref.at[gvec_id, pl.ds(chunk * y_chunk, y_chunk), window],
            send_sem=fsend.at[step, chunk], recv_sem=frecv.at[step, chunk],
            device_id=gvec_peer(step), device_id_type=MESH,
        )

    start_rows, wait_rows = broadcast(0, row_ref, rows_ref)
    lax.fori_loop(0, ahead, forward, 0)
    pl.semaphore_wait(barrier, total - 1)
    start_rows()
    if ahead:
        for step in range(1, gvec_size):
            lead_copy(step).start()
    lax.fori_loop(ahead, pieces, forward, 0)
    for chunk in range(chunks):
        for step in range(1, gvec_size):
            forward_copy(step, chunk).start()
    own_copy = pltpu.make_async_copy(
        sect_ref.at[pl.ds(gvec_id * y_share, y_share)], held_ref.at[gvec_id], own_sem.at[0]
    )
    own_copy.start()

    local_copy.wait()
    x_block = 16

    def turn_local(index, carry):
        window = pl.ds(pl.multiple_of(index * x_block, x_block), x_block)
        stage_ref[pl.ds(0, x_block * y_share)] = (
            local_ref[window].astype(F32).reshape(x_block * y_share, extent)
        )

        def turn(outer, inner_carry):
            for inner in range(8):
                y = outer * 8 + inner
                field_ref[y, window] = stage_ref[pl.ds(y, x_block, stride=y_share)]
            return inner_carry

        lax.fori_loop(0, y_share // 8, turn, 0)
        return carry

    lax.fori_loop(0, extent // x_block, turn_local, 0)

    wait_rows(1, total)
    rows = rows_ref[:, 0, :]
    count = rows[:, 4 * cap : 4 * cap + 1]
    count_wide = jnp.broadcast_to(count, (total, live_total))
    offset = jnp.dot(group_ref[1], count_wide, precision=HIGH, preferred_element_type=F32)
    order = iota((total, live_total), 1).astype(F32)
    holds = ((order >= offset) & (order < offset + count_wide)).astype(F32)
    slot_at = jnp.sum(holds * (order - offset), axis=0, keepdims=True)
    spread_rows = lax.dot_general(
        rows, holds, (((0,), (0,)), ((), ())), precision=HIGH, preferred_element_type=F32
    )
    here = (iota((cap, live_total), 0).astype(F32) == slot_at).astype(F32)
    centre = [
        jnp.sum(spread_rows[k * cap : (k + 1) * cap] * here, axis=0, keepdims=True) for k in range(4)
    ]
    mine = (iota((total, 1), 0) == me).astype(F32)
    own_offset = jnp.sum(mine * offset[:, :1], axis=0, keepdims=True)
    place_ref[...] = jnp.broadcast_to(own_offset, place_ref.shape)

    x_points = iota((extent, live_total), 0).astype(F32)
    y_points = (iota((y_share, live_total), 0) + gvec_id * y_share).astype(F32)
    for k, fraction in enumerate(sigma_fractions):
        exponent = 0.5 / (extent * fraction) ** 2
        window = slice(k * live_total, (k + 1) * live_total)
        scaled = kernel_weights[k] * centre[3]
        scale_ref[:, window] = scaled
        away = x_points - centre[0]
        value = jnp.exp(-exponent * away * away)
        xg_ref[:, window] = value
        xh_ref[:, window] = 2.0 * exponent * away * value
        away = y_points - centre[1]
        value = jnp.exp(-exponent * away * away)
        slope = 2.0 * exponent * away * value
        yg_ref[:, window] = value
        for part in range(live_total // 128):
            y_ref[0, k * live_total // 128 + part] = value[:, part * 128 : (part + 1) * 128]
            y_ref[1, k * live_total // 128 + part] = slope[:, part * 128 : (part + 1) * 128]
        away = x_points - centre[2]
        value = jnp.exp(-exponent * away * away)
        depth_ref[window] = jnp.transpose(scaled * value).astype(BF16)
        zg_ref[:, window] = value.astype(BF16)
        zh_ref[:, window] = (2.0 * exponent * away * value).astype(BF16)

    block = min(width, 512)

    field_rows = 4

    def add_field(index, carry):
        value = None
        for part in range(width // block):
            window = slice(part * block, (part + 1) * block)
            plane = jnp.concatenate(
                [
                    (xg_ref[:, window] * yg_ref[pl.ds(index * field_rows + side, 1), window]).astype(BF16)
                    for side in range(field_rows)
                ],
                axis=0,
            )
            term = dot(plane, depth_ref[window])
            value = term if value is None else value + term
        value = value.astype(BF16).astype(F32)
        for side in range(field_rows):
            field_ref[index * field_rows + side] += value[side * extent : (side + 1) * extent]
        return carry

    lax.fori_loop(0, y_share // field_rows, add_field, 0)

    def back_copy(step, chunk, part):
        owner = gvec_at[step]
        return pltpu.make_async_remote_copy(
            src_ref=going_ref.at[chunk, pl.ds(owner * x_local + part * piece, piece)],
            dst_ref=back_ref.at[gvec_id, chunk, pl.ds(part * piece, piece)],
            send_sem=bsend.at[step, chunk, part], recv_sem=brecv.at[step, chunk, part],
            device_id=gvec_peer(step), device_id_type=MESH,
        )

    def own_back(chunk):
        return pltpu.make_async_copy(
            going_ref.at[chunk, pl.ds(gvec_id * x_local, x_local)],
            back_ref.at[gvec_id, chunk], own_sem.at[1 + chunk],
        )

    own_copy.wait()

    if ahead:
        for step in range(1, gvec_size):
            lead_copy(step).wait_recv()

    def middle(chunk, carry):
        for step in range(1, gvec_size):
            forward_copy(step, chunk).wait_recv()
        for pair in range(y_chunk // 2):
            first = chunk * y_chunk + 2 * pair
            both = jnp.concatenate(
                [
                    jnp.concatenate([held_ref[source, first + side] for source in range(gvec_size)], axis=0)
                    for side in range(2)
                ],
                axis=1,
            )
            wide = dot(cos_ref[0], both).astype(BF16).astype(F32)
            square = (wide * wide).astype(BF16)
            dens_ref[first] = square[:, :extent]
            dens_ref[first + 1] = square[:, extent:]
            fields = jnp.concatenate([field_ref[first], field_ref[first + 1]], axis=1)
            result = dot(cos_ref[1], (fields * wide).astype(BF16))
            stage_ref[pl.ds(2 * pair * extent, extent)] = result[:, :extent]
            stage_ref[pl.ds((2 * pair + 1) * extent, extent)] = result[:, extent:]

        def spread(outer, inner_carry):
            for inner in range(8):
                a = outer * 8 + inner
                going_ref[chunk, a] = stage_ref[pl.ds(a, y_chunk, stride=extent)].astype(BF16)
            return inner_carry

        lax.fori_loop(0, extent // 8, spread, 0)
        for part in range(pieces):
            for step in range(1, gvec_size):
                back_copy(step, chunk, part).start()
        own_back(chunk).start()
        return carry

    lax.fori_loop(0, chunks, middle, 0)

    q_wave = iota((extent, extent), 0).astype(F32) * wave_step
    l_wave = iota((extent, extent), 1).astype(F32) * wave_step
    plane_kinetic = 0.5 * (q_wave * q_wave + l_wave * l_wave)
    moment_ref[...] = jnp.zeros_like(moment_ref)

    def x_wave_of(a):
        return jnp.full((1, 1), gvec_id * x_local + a, jnp.int32).astype(F32) * wave_step

    def coefficients(index, carry):
        zero, one, two = 0.0, 0.0, 0.0
        for inner in range(4):
            a = index * 4 + inner
            wide = coeff_ref[a].astype(F32)
            x_wave = x_wave_of(a)
            square = wide * wide
            by_x = square * x_wave
            zero, one, two = zero + square, one + by_x, two + by_x * x_wave
            recip_ref[a] = step_size / (1.0 + 0.5 * x_wave * x_wave + plane_kinetic)
        moment_ref[0] += zero
        moment_ref[1] += one
        moment_ref[2] += two
        return carry

    lax.fori_loop(0, x_local // 4, coefficients, 0)
    group_id = band_id * dom_size + dom_id
    shifted = jnp.full((1, 1), group_id, jnp.int32).astype(F32) - 0.5 * band_total
    weight = 2.0 / (1.0 + jnp.exp(shifted / (0.125 * band_total)))
    terms = (
        moment_ref[2],
        moment_ref[0] * q_wave * q_wave,
        moment_ref[0] * l_wave * l_wave,
        moment_ref[1] * q_wave,
        moment_ref[1] * l_wave,
        moment_ref[0] * q_wave * l_wave,
    )
    stress = [weight * total_of(term) / cells for term in terms]

    x_part = 32

    def project(index, carry):
        at = pl.ds(pl.multiple_of(index * 128, 128), 128)
        tables = jnp.concatenate([zg_ref[:, at], zh_ref[:, at]], axis=1)

        def over_x(x_at, sums):
            x_window = pl.ds(pl.multiple_of(x_at * x_part, x_part), x_part)
            result = dot(dens_ref[:, x_window].reshape(y_share * x_part, extent), tables)
            along, slope, deep = 0.0, 0.0, 0.0
            for y in range(y_share):
                rows_at = slice(y * x_part, (y + 1) * x_part)
                value, derivative = y_ref[0, index, pl.ds(y, 1)], y_ref[1, index, pl.ds(y, 1)]
                along = along + result[rows_at, :128] * value
                slope = slope + result[rows_at, :128] * derivative
                deep = deep + result[rows_at, 128:] * value
            value, derivative = xg_ref[x_window, at], xh_ref[x_window, at]
            terms = (derivative * along, value * slope, value * deep, value * along)
            return tuple(
                old + jnp.sum(term.reshape(-1, 8, 128), axis=0) for old, term in zip(sums, terms)
            )

        start = tuple(jnp.zeros((8, 128), F32) for _ in range(4))
        sums = lax.fori_loop(0, extent // x_part, over_x, start)
        for at_sum in range(4):
            total_row = jnp.sum(sums[at_sum], axis=0, keepdims=True)
            proj_ref[at_sum : at_sum + 1, at] = total_row * scale_ref[:, at]
        return carry

    lax.fori_loop(0, width // 128, project, 0)
    folded = jnp.zeros((4, live_total), F32)
    for k in range(len(kernel_weights)):
        folded = folded + proj_ref[:, k * live_total : (k + 1) * live_total]
    tile_ref[0:3] = (-force_unit * weight) * folded[0:3]
    embedding = weight * jnp.sum(folded[3:4], axis=1, keepdims=True) / cells
    line = jnp.zeros((1, live_total), F32)
    tile_lane = iota((1, live_total), 1)
    for at, value in enumerate(stress + [embedding]):
        line = jnp.where(tile_lane == at, value, line)
    tile_ref[3:4] = line
    tiles_ref[me] = tile_ref[...]
    start_tiles, wait_tiles = broadcast(1, tile_ref, tiles_ref)
    start_tiles()

    for chunk in range(chunks):
        own_back(chunk).wait()
    norms, inners, squares = [], [], []

    def force_to_atoms():
        wait_tiles(1, total)
        summed = tiles_ref[0]
        for source in range(1, total):
            summed = summed + tiles_ref[source]
        slot_lanes = (iota((live_total, 128), 0).astype(F32) - place_ref[0:1, 0:1]) == iota(
            (live_total, 128), 1
        ).astype(F32)
        slot_lanes = slot_lanes & (iota((live_total, 128), 1) < live)
        slot_force = jnp.dot(summed, slot_lanes.astype(F32), precision=HIGH, preferred_element_type=F32)
        near_column = jnp.full((128, 1), -1, jnp.int32)
        for slot in range(cap):
            near_column = jnp.where(iota((128, 1), 0) == slot, near_ref[slot], near_column)
        at_atom = (iota((128, atoms), 1) == near_column).astype(F32)
        atom_force = jnp.dot(slot_force, at_atom, precision=HIGH, preferred_element_type=F32)
        force_out[...] = atom_force[0:3]
        return summed

    for part in range(pieces):
        if part == pieces - 1:
            summed = force_to_atoms()
        for chunk in range(chunks):
            for step in range(1, gvec_size):
                back_copy(step, chunk, part).wait_recv()

        def image_of(index, carry):
            norm, inner = carry
            for pair in range(2):
                first = part * piece + 4 * index + 2 * pair
                both = jnp.concatenate(
                    [
                        jnp.concatenate(
                            [
                                back_ref[source, chunk, first + side]
                                for source in range(gvec_size)
                                for chunk in range(chunks)
                            ],
                            axis=0,
                        )
                        for side in range(2)
                    ],
                    axis=1,
                )
                section = dot(cos_ref[1], both).astype(BF16)
                waves = dot(section, diag_ref[1])
                for side in range(2):
                    a = first + side
                    wide = coeff_ref[a].astype(F32)
                    x_wave = x_wave_of(a)
                    image = (0.5 * x_wave * x_wave + plane_kinetic) * wide
                    image = image + waves[:, side * extent : (side + 1) * extent]
                    image_ref[a] = image
                    norm = norm + jnp.sum((wide * wide).reshape(-1, 8, extent), axis=0)
                    inner = inner + jnp.sum((wide * image).reshape(-1, 8, extent), axis=0)
            return norm, inner

        empty = jnp.zeros((8, extent), F32)
        norm, inner = lax.fori_loop(0, piece // 4, image_of, (empty, empty))
        norm, inner = total_of(norm), total_of(inner)
        filled = norm > 0.0
        energy = jnp.where(filled, inner / jnp.where(filled, norm, 1.0), 0.0)

        def residual_of(index, square):
            for side in range(4):
                a = part * piece + 4 * index + side
                wide = coeff_ref[a].astype(F32)
                image = image_ref[a]
                residual = image - energy * wide
                square = square + jnp.sum((residual * residual).reshape(-1, 8, extent), axis=0)
                image_ref[a] = wide - image * recip_ref[a]
            return square

        square = total_of(lax.fori_loop(0, piece // 4, residual_of, empty))
        norms.append(norm)
        inners.append(inner)
        squares.append(square)

    def merged(parts):
        norm = sum(part[0] for part in parts)
        inner = sum(part[1] for part in parts)
        filled = norm > 0.0
        energy = jnp.where(filled, inner / jnp.where(filled, norm, 1.0), 0.0)
        square = 0.0
        for part_norm, part_inner, part_square in parts:
            filled = part_norm > 0.0
            part_energy = jnp.where(filled, part_inner / jnp.where(filled, part_norm, 1.0), 0.0)
            away = part_energy - energy
            square = square + part_square + away * away * part_norm
        return norm, inner, square

    own = merged(list(zip(norms, inners, squares)))
    last_lane = iota(last_ref.shape, 1)
    last = jnp.zeros(last_ref.shape, F32)
    for at, value in enumerate(own):
        last = jnp.where(last_lane == at, value, last)
    last_ref[...] = last
    lasts_ref[me] = last
    start_last, wait_last = broadcast(2, last_ref, lasts_ref)
    start_last()
    wait_last(1, gvec_size)
    parts = []
    for source in range(gvec_size):
        other = lasts_ref[(band_id * gvec_size + source) * dom_size + dom_id]
        parts.append(tuple(other[:, at : at + 1] for at in range(3)))
    norm, inner, square = merged(parts)
    energy = inner / norm

    def update(index, carry):
        for side in range(4):
            a = index * 4 + side
            wide = coeff_ref[a].astype(F32)
            waves_ref[0, a] = (image_ref[a] + energy * (wide * recip_ref[a])).astype(BF16)
        return carry

    lax.fori_loop(0, x_local // 4, update, 0)

    wait_last(gvec_size, total)
    lasts = lasts_ref[:, 0, :]
    both = jnp.dot(group_ref[0], lasts, precision=HIGH, preferred_element_type=F32)
    band_energy = both[:, 1:2] / both[:, 0:1]
    occupied = 2.0 / (1.0 + jnp.exp((band_ref[...] - 0.5 * band_total) / (0.125 * band_total)))
    band_sum = jnp.sum(occupied * band_energy, axis=0, keepdims=True) / float(gvec_size * band_total)
    misc_lane = iota((1, 128), 1)
    misc_ref[0:1] = jnp.broadcast_to(energy, (1, 128))
    misc_ref[1:2] = jnp.broadcast_to(square / norm, (1, 128))
    misc_ref[2:3] = jnp.where(misc_lane == 7, band_sum, summed[3:4, :128])
    misc_ref[3:8] = jnp.zeros((5, 128), F32)

    for step in range(1, gvec_size):
        if ahead:
            lead_copy(step).wait_send()
        for chunk in range(chunks):
            forward_copy(step, chunk).wait_send()
            for part in range(pieces):
                back_copy(step, chunk, part).wait_send()


def per_device(sizes, coeffs, v_local, atom_pos, atom_charge, near_list, live_count):
    gvec_size = sizes[1]
    total = sizes[0] * sizes[1] * sizes[2]
    local_bands, x_local, extent, _ = coeffs.shape
    assert local_bands == 1
    y_share = v_local.shape[1]
    cap = near_list.shape[0]
    atoms = atom_pos.shape[1]
    live_total = total * cap // 4
    width = len(kernel_weights) * live_total
    y_chunk = 16 if y_share % 16 == 0 else y_share
    chunks = y_share // y_chunk
    piece = 16 if x_local % 16 == 0 else x_local
    pieces = x_local // piece
    lanes = -(-(4 * cap + 1) // 128) * 128
    pair, diagonal = constant_tables(extent)
    groups, bands = group_tables(sizes)
    vmem = pl.BlockSpec(memory_space=pltpu.VMEM)
    smem = pl.BlockSpec(memory_space=pltpu.SMEM)
    hbm = pl.BlockSpec(memory_space=pltpu.HBM)
    plan = (x_local, extent, y_share, cap, live_total, atoms)
    deep = max(piece, y_chunk, 16)
    dma = pltpu.SemaphoreType.DMA
    operands = [
        pltpu.with_memory_space_constraint(operand, pltpu.HBM)
        for operand in (
            near_list, atom_pos, atom_charge.reshape(1, atoms), jnp.asarray(pair),
            jnp.asarray(diagonal), jnp.asarray(groups), jnp.asarray(bands), coeffs, v_local,
        )
    ]
    waves_new, atom_force, misc = pl.pallas_call(
        functools.partial(step_kernel, sizes, plan),
        out_shape=(
            jax.ShapeDtypeStruct(coeffs.shape, BF16),
            jax.ShapeDtypeStruct((3, atoms), F32),
            jax.ShapeDtypeStruct((8, 128), F32),
        ),
        in_specs=[hbm, smem] + [hbm] * 8,
        out_specs=(vmem, vmem, vmem),
        scratch_shapes=[
            pltpu.SMEM(near_list.shape, jnp.int32),
            pltpu.VMEM(atom_pos.shape, F32),
            pltpu.VMEM((1, atoms), F32),
            pltpu.VMEM(pair.shape, BF16),
            pltpu.VMEM(diagonal.shape, BF16),
            pltpu.VMEM(groups.shape, F32),
            pltpu.VMEM(bands.shape, F32),
            pltpu.VMEM((x_local, extent, extent), BF16),
            pltpu.VMEM(v_local.shape, BF16),
            pltpu.VMEM((deep * extent, extent), F32),
            pltpu.VMEM((extent, x_local, extent), BF16),
            pltpu.VMEM((gvec_size, y_share, x_local, extent), BF16),
            pltpu.VMEM((y_share, extent, extent), F32),
            pltpu.VMEM((y_share, extent, extent), BF16),
            pltpu.VMEM((chunks, extent, y_chunk, extent), BF16),
            pltpu.VMEM((gvec_size, chunks, x_local, y_chunk, extent), BF16),
            pltpu.VMEM((x_local, extent, extent), F32),
            pltpu.VMEM((x_local, extent, extent), F32),
            pltpu.VMEM((3, extent, extent), F32),
            pltpu.VMEM((1, lanes), F32),
            pltpu.VMEM((total, 1, lanes), F32),
            pltpu.VMEM((4, live_total), F32),
            pltpu.VMEM((total, 4, live_total), F32),
            pltpu.VMEM((1, 128), F32),
            pltpu.VMEM((total, 1, 128), F32),
            pltpu.VMEM((extent, width), F32),
            pltpu.VMEM((extent, width), F32),
            pltpu.VMEM((y_share, width), F32),
            pltpu.VMEM((2, width // 128, y_share, 128), F32),
            pltpu.VMEM((width, extent), BF16),
            pltpu.VMEM((extent, width), BF16),
            pltpu.VMEM((extent, width), BF16),
            pltpu.VMEM((1, width), F32),
            pltpu.VMEM((8, 128), F32),
            pltpu.VMEM((4, width), F32),
            dma((pieces,)),
            dma,
            dma((7,)),
            dma((1 + chunks,)),
            dma((gvec_size, chunks + 1)),
            dma((gvec_size, chunks + 1)),
            dma((gvec_size, chunks, pieces)),
            dma((gvec_size, chunks, pieces)),
            dma((3, total)),
            dma((3, total)),
        ],
        compiler_params=pltpu.CompilerParams(
            collective_id=0, has_side_effects=True, vmem_limit_bytes=36 * 1024 * 1024
        ),
        name="step",
    )(operands[0], live_count, *operands[1:])
    return (waves_new, misc[0, :1], misc[1, :1], atom_force, misc[2, :8])


def solution(mesh):
    sizes = (mesh.shape["band"], mesh.shape["gvec"], mesh.shape["dom"])
    return jax.shard_map(
        functools.partial(per_device, sizes),
        mesh=mesh,
        in_specs=(
            P(("band", "dom"), "gvec", None, None),
            P(None, "gvec", None),
            P(None, ("band", "gvec", "dom")),
            P(("band", "gvec", "dom")),
            P(("band", "gvec", "dom")),
            P(("band", "gvec", "dom")),
        ),
        out_specs=(
            P(("band", "dom"), "gvec", None, None),
            P(("band", "dom")),
            P(("band", "dom")),
            P(None, ("band", "gvec", "dom")),
            P(),
        ),
        check_vma=False,
    )
```

```python
import functools

import jax
import jax.numpy as jnp
import numpy as np
from jax import lax
from jax.experimental import pallas as pl
from jax.experimental.pallas import tpu as pltpu
from jax.sharding import PartitionSpec as P

sigma_fractions = (1.0 / 32.0, 1.0 / 16.0, 1.0 / 8.0, 1.0 / 4.0)
kernel_weights = (1.0, 0.5, 0.25, 0.125)
force_unit = 1.0 / 4096.0
step_size = 0.5
MESH = pl.DeviceIdType.MESH
F32 = jnp.float32
BF16 = jnp.bfloat16
HIGH = lax.Precision.HIGHEST


def cosine_table(length):
    points = np.arange(length).astype(np.float32)
    angles = np.float32(np.pi) * (points[:, None] + np.float32(0.5)) * points[None, :] / np.float32(length)
    scales = np.where(points == 0.0, np.sqrt(1.0 / length), np.sqrt(2.0 / length)).astype(np.float32)
    return (np.cos(angles.astype(np.float64)).astype(np.float32) * scales[None, :]).astype(jnp.bfloat16)


def constant_tables(length):
    cosines = cosine_table(length)
    zero = np.zeros_like(cosines)
    pair = np.stack([cosines, cosines.T])
    diagonal = np.stack(
        [np.block([[cosines.T, zero], [zero, cosines.T]]), np.block([[cosines, zero], [zero, cosines]])]
    )
    return pair, diagonal


def dot(left, right):
    return jnp.dot(left, right, preferred_element_type=F32)


def total_of(value):
    return jnp.sum(jnp.sum(value, axis=0, keepdims=True), axis=1, keepdims=True)


def iota(shape, axis):
    return lax.broadcasted_iota(jnp.int32, shape, axis)


def step_kernel(
    sizes, plan,
    near_hbm, live_ref, pos_hbm, charge_hbm, cos_hbm, diag_hbm, group_hbm, coeff_hbm, local_hbm,
    waves_ref, force_out, misc_ref,
    near_ref, pos_ref, charge_ref, cos_ref, diag_ref, group_ref, coeff_ref, local_ref, stage_ref, sect_ref, held_ref, field_ref, dens_ref, going_ref, back_ref,
    image_ref, recip_ref, moment_ref, row_ref, rows_ref, tile_ref, tiles_ref, last_ref, lasts_ref,
    xg_ref, xh_ref, yg_ref, y_ref, depth_ref, zg_ref, zh_ref, scale_ref, place_ref, proj_ref,
    load_sem, local_sem, small_sem, own_sem, fsend, frecv, bsend, brecv, csend, crecv,
):
    band_size, gvec_size, dom_size = sizes
    total = band_size * gvec_size * dom_size
    x_local, extent, y_share, cap, live_total, atoms = plan
    band_id, gvec_id, dom_id = lax.axis_index("band"), lax.axis_index("gvec"), lax.axis_index("dom")
    me = (band_id * gvec_size + gvec_id) * dom_size + dom_id
    band_total = band_size * dom_size
    width = len(kernel_weights) * live_total
    cells = float(extent**3)
    wave_step = np.float32(np.pi / extent)
    y_chunk = 16 if y_share % 16 == 0 else y_share
    chunks = y_share // y_chunk
    piece = 16 if x_local % 16 == 0 else x_local
    pieces = x_local // piece
    grain = 8 if x_local % 8 == 0 else x_local
    grains = x_local // grain
    early = max(chunks - 2, 0)
    barrier = pltpu.get_barrier_semaphore()

    def load_of(part):
        window = pl.ds(part * piece, piece)
        return pltpu.make_async_copy(coeff_hbm.at[0, window], coeff_ref.at[window], load_sem.at[part])

    smalls = [
        pltpu.make_async_copy(source, target, small_sem.at[at])
        for at, (source, target) in enumerate(
            (
                (near_hbm, near_ref), (pos_hbm, pos_ref), (charge_hbm, charge_ref),
                (cos_hbm, cos_ref), (diag_hbm, diag_ref), (group_hbm, group_ref),
            )
        )
    ]
    for copy in smalls:
        copy.start()
    for part in range(pieces):
        load_of(part).start()
    local_copy = pltpu.make_async_copy(local_hbm, local_ref, local_sem)
    local_copy.start()

    band_at = [lax.rem(band_id + shift, band_size) for shift in range(band_size)]
    gvec_at = [lax.rem(gvec_id + shift, gvec_size) for shift in range(gvec_size)]
    dom_at = [lax.rem(dom_id + shift, dom_size) for shift in range(dom_size)]

    def peer_of(step):
        outer = step // gvec_size
        return band_at[outer // dom_size], gvec_at[step % gvec_size], dom_at[outer % dom_size]

    for step in range(1, total):
        pl.semaphore_signal(barrier, inc=1, device_id=peer_of(step), device_id_type=MESH)

    def broadcast(kind, src, dst):
        def copy_of(step):
            return pltpu.make_async_remote_copy(
                src_ref=src, dst_ref=dst.at[me],
                send_sem=csend.at[kind, step], recv_sem=crecv.at[kind, step],
                device_id=peer_of(step), device_id_type=MESH,
            )

        def start():
            for step in range(1, total):
                copy_of(step).start()

        def wait(first, stop):
            for step in range(first, stop):
                copy_of(step).wait()

        return start, wait

    group = piece
    smalls[3].wait()
    smalls[4].wait()

    def forward(index, carry):
        load_of(index).wait()
        for pair in range(group // 2):
            first = index * group + 2 * pair
            both = jnp.concatenate([coeff_ref[first], coeff_ref[first + 1]], axis=1)
            section = dot(both, diag_ref[0]).astype(BF16)
            result = dot(cos_ref[0], section)
            stage_ref[pl.ds(2 * pair * extent, extent)] = result[:, :extent]
            stage_ref[pl.ds((2 * pair + 1) * extent, extent)] = result[:, extent:]
        window = pl.ds(pl.multiple_of(index * group, group), group)

        def spread(outer, inner_carry):
            for inner in range(8):
                y = outer * 8 + inner
                sect_ref[y, window] = stage_ref[pl.ds(y, group, stride=extent)].astype(BF16)
            return inner_carry

        lax.fori_loop(0, extent // 8, spread, 0)
        return carry

    ahead = pieces // 2

    def gvec_peer(step):
        return (band_id, gvec_at[step], dom_id)

    def lead_copy(step, part):
        window = pl.ds(part * piece, piece)
        return pltpu.make_async_remote_copy(
            src_ref=sect_ref.at[pl.ds(gvec_at[step] * y_share, y_share), window],
            dst_ref=held_ref.at[gvec_id, :, window],
            send_sem=fsend.at[step, chunks + part], recv_sem=frecv.at[step, chunks + part],
            device_id=gvec_peer(step), device_id_type=MESH,
        )

    def forward_copy(step, chunk):
        owner = gvec_at[step]
        window = pl.ds(ahead * piece, x_local - ahead * piece)
        return pltpu.make_async_remote_copy(
            src_ref=sect_ref.at[pl.ds(owner * y_share + chunk * y_chunk, y_chunk), window],
            dst_ref=held_ref.at[gvec_id, pl.ds(chunk * y_chunk, y_chunk), window],
            send_sem=fsend.at[step, chunk], recv_sem=frecv.at[step, chunk],
            device_id=gvec_peer(step), device_id_type=MESH,
        )

    if ahead:
        forward(0, 0)
    pl.semaphore_wait(barrier, total - 1)
    if ahead:
        for step in range(1, gvec_size):
            lead_copy(step, 0).start()

    for at in (0, 1, 2, 5):
        smalls[at].wait()

    lanes = row_ref.shape[1]
    lane = iota((1, lanes), 1)
    near_row = jnp.full((1, lanes), -1, jnp.int32)
    for quantity in range(4):
        for slot in range(cap):
            near_row = jnp.where(lane == quantity * cap + slot, near_ref[slot], near_row)
    live = live_ref[0]
    chosen = (iota((atoms, lanes), 0) == near_row).astype(F32)
    picked_pos = jnp.dot(pos_ref[...], chosen, precision=HIGH, preferred_element_type=F32)
    picked_charge = jnp.dot(charge_ref[...], chosen, precision=HIGH, preferred_element_type=F32)
    row = jnp.zeros((1, lanes), F32)
    for quantity in range(3):
        part = (lane >= quantity * cap) & (lane < (quantity + 1) * cap)
        row = jnp.where(part, picked_pos[quantity : quantity + 1], row)
    part = (lane >= 3 * cap) & (lane < 3 * cap + live) & (lane < 4 * cap)
    row = jnp.where(part, picked_charge, row)
    row = jnp.where(lane == 4 * cap, live.astype(F32), row)
    row_ref[...] = row
    rows_ref[me] = row
    start_rows, wait_rows = broadcast(0, row_ref, rows_ref)
    start_rows()

    def lead(part, carry):
        forward(part, carry)
        for step in range(1, gvec_size):
            lead_copy(step, part).start()
        return carry

    lax.fori_loop(1, ahead, lead, 0)
    lax.fori_loop(ahead, pieces, forward, 0)
    for chunk in range(chunks):
        for step in range(1, gvec_size):
            forward_copy(step, chunk).start()
    own_copy = pltpu.make_async_copy(
        sect_ref.at[pl.ds(gvec_id * y_share, y_share)], held_ref.at[gvec_id], own_sem.at[0]
    )
    own_copy.start()

    local_copy.wait()
    x_block = 16

    def turn_local(index, carry):
        window = pl.ds(pl.multiple_of(index * x_block, x_block), x_block)
        stage_ref[pl.ds(0, x_block * y_share)] = (
            local_ref[window].astype(F32).reshape(x_block * y_share, extent)
        )

        def turn(outer, inner_carry):
            for inner in range(8):
                y = outer * 8 + inner
                field_ref[y, window] = stage_ref[pl.ds(y, x_block, stride=y_share)]
            return inner_carry

        lax.fori_loop(0, y_share // 8, turn, 0)
        return carry

    lax.fori_loop(0, extent // x_block, turn_local, 0)

    wait_rows(1, total)
    rows = rows_ref[:, 0, :]
    count = rows[:, 4 * cap : 4 * cap + 1]
    count_wide = jnp.broadcast_to(count, (total, live_total))
    offset = jnp.dot(group_ref[...], count_wide, precision=HIGH, preferred_element_type=F32)
    order = iota((total, live_total), 1).astype(F32)
    holds = ((order >= offset) & (order < offset + count_wide)).astype(F32)
    slot_at = jnp.sum(holds * (order - offset), axis=0, keepdims=True)
    spread_rows = lax.dot_general(
        rows, holds, (((0,), (0,)), ((), ())), precision=HIGH, preferred_element_type=F32
    )
    here = (iota((cap, live_total), 0).astype(F32) == slot_at).astype(F32)
    centre = [
        jnp.sum(spread_rows[k * cap : (k + 1) * cap] * here, axis=0, keepdims=True) for k in range(4)
    ]
    mine = (iota((total, 1), 0) == me).astype(F32)
    own_offset = jnp.sum(mine * offset[:, :1], axis=0, keepdims=True)
    place_ref[...] = jnp.broadcast_to(own_offset, place_ref.shape)

    x_points = iota((extent, live_total), 0).astype(F32)
    y_points = (iota((y_share, live_total), 0) + gvec_id * y_share).astype(F32)
    for k, fraction in enumerate(sigma_fractions):
        exponent = 0.5 / (extent * fraction) ** 2
        window = slice(k * live_total, (k + 1) * live_total)
        scaled = kernel_weights[k] * centre[3]
        scale_ref[:, window] = scaled
        away = x_points - centre[0]
        value = jnp.exp(-exponent * away * away)
        xg_ref[:, window] = value
        xh_ref[:, window] = 2.0 * exponent * away * value
        away = y_points - centre[1]
        value = jnp.exp(-exponent * away * away)
        slope = 2.0 * exponent * away * value
        yg_ref[:, window] = value
        for part in range(live_total // 128):
            y_ref[0, k * live_total // 128 + part] = value[:, part * 128 : (part + 1) * 128]
            y_ref[1, k * live_total // 128 + part] = slope[:, part * 128 : (part + 1) * 128]
        away = x_points - centre[2]
        value = jnp.exp(-exponent * away * away)
        depth_ref[window] = jnp.transpose(scaled * value).astype(BF16)
        zg_ref[:, window] = value.astype(BF16)
        zh_ref[:, window] = (2.0 * exponent * away * value).astype(BF16)

    block = min(width, 512)

    field_rows = 4

    def add_field(index, carry):
        value = None
        for part in range(width // block):
            window = slice(part * block, (part + 1) * block)
            plane = jnp.concatenate(
                [
                    (xg_ref[:, window] * yg_ref[pl.ds(index * field_rows + side, 1), window]).astype(BF16)
                    for side in range(field_rows)
                ],
                axis=0,
            )
            term = dot(plane, depth_ref[window])
            value = term if value is None else value + term
        value = value.astype(BF16).astype(F32)
        for side in range(field_rows):
            field_ref[index * field_rows + side] += value[side * extent : (side + 1) * extent]
        return carry

    lax.fori_loop(0, y_share // field_rows, add_field, 0)

    def back_copy(step, chunk, part):
        owner = gvec_at[step]
        return pltpu.make_async_remote_copy(
            src_ref=going_ref.at[chunk, pl.ds(owner * x_local + part * grain, grain)],
            dst_ref=back_ref.at[gvec_id, chunk, pl.ds(part * grain, grain)],
            send_sem=bsend.at[step, chunk, part], recv_sem=brecv.at[step, chunk, part],
            device_id=gvec_peer(step), device_id_type=MESH,
        )

    def own_back(chunk):
        return pltpu.make_async_copy(
            going_ref.at[chunk, pl.ds(gvec_id * x_local, x_local)],
            back_ref.at[gvec_id, chunk], own_sem.at[1 + chunk],
        )

    own_copy.wait()

    for step in range(1, gvec_size):
        for part in range(ahead):
            lead_copy(step, part).wait_recv()

    def middle(chunk, carry):
        for step in range(1, gvec_size):
            forward_copy(step, chunk).wait_recv()
        for pair in range(y_chunk // 2):
            first = chunk * y_chunk + 2 * pair
            both = jnp.concatenate(
                [
                    jnp.concatenate([held_ref[source, first + side] for source in range(gvec_size)], axis=0)
                    for side in range(2)
                ],
                axis=1,
            )
            wide = dot(cos_ref[0], both).astype(BF16).astype(F32)
            square = (wide * wide).astype(BF16)
            dens_ref[first] = square[:, :extent]
            dens_ref[first + 1] = square[:, extent:]
            fields = jnp.concatenate([field_ref[first], field_ref[first + 1]], axis=1)
            result = dot(cos_ref[1], (fields * wide).astype(BF16))
            stage_ref[pl.ds(2 * pair * extent, extent)] = result[:, :extent]
            stage_ref[pl.ds((2 * pair + 1) * extent, extent)] = result[:, extent:]

        def spread(outer, inner_carry):
            for inner in range(8):
                a = outer * 8 + inner
                going_ref[chunk, a] = stage_ref[pl.ds(a, y_chunk, stride=extent)].astype(BF16)
            return inner_carry

        lax.fori_loop(0, extent // 8, spread, 0)
        own_back(chunk).start()
        return carry

    def middle_early(chunk, carry):
        middle(chunk, carry)
        for part in range(grains):
            for step in range(1, gvec_size):
                back_copy(step, chunk, part).start()
        return carry

    lax.fori_loop(0, early, middle_early, 0)
    lax.fori_loop(early, chunks, middle, 0)

    def send_late(part, carry):
        for chunk in range(early, chunks):
            for step in range(1, gvec_size):
                back_copy(step, chunk, part).start()
        return carry

    lax.fori_loop(0, grains, send_late, 0)

    q_wave = iota((extent, extent), 0).astype(F32) * wave_step
    l_wave = iota((extent, extent), 1).astype(F32) * wave_step
    plane_kinetic = 0.5 * (q_wave * q_wave + l_wave * l_wave)
    moment_ref[...] = jnp.zeros_like(moment_ref)

    def x_wave_of(a):
        return jnp.full((1, 1), gvec_id * x_local + a, jnp.int32).astype(F32) * wave_step

    def coefficients(index, carry):
        zero, one, two = 0.0, 0.0, 0.0
        for inner in range(4):
            a = index * 4 + inner
            wide = coeff_ref[a].astype(F32)
            x_wave = x_wave_of(a)
            square = wide * wide
            by_x = square * x_wave
            zero, one, two = zero + square, one + by_x, two + by_x * x_wave
            recip_ref[a] = step_size / (1.0 + 0.5 * x_wave * x_wave + plane_kinetic)
        moment_ref[0] += zero
        moment_ref[1] += one
        moment_ref[2] += two
        return carry

    lax.fori_loop(0, x_local // 4, coefficients, 0)
    group_id = band_id * dom_size + dom_id
    shifted = jnp.full((1, 1), group_id, jnp.int32).astype(F32) - 0.5 * band_total
    weight = 2.0 / (1.0 + jnp.exp(shifted / (0.125 * band_total)))
    terms = (
        moment_ref[2],
        moment_ref[0] * q_wave * q_wave,
        moment_ref[0] * l_wave * l_wave,
        moment_ref[1] * q_wave,
        moment_ref[1] * l_wave,
        moment_ref[0] * q_wave * l_wave,
    )
    stress = [weight * total_of(term) / cells for term in terms]

    x_part = 32

    def project(index, carry):
        at = pl.ds(pl.multiple_of(index * 128, 128), 128)
        tables = jnp.concatenate([zg_ref[:, at], zh_ref[:, at]], axis=1)

        def over_x(x_at, sums):
            x_window = pl.ds(pl.multiple_of(x_at * x_part, x_part), x_part)
            result = dot(dens_ref[:, x_window].reshape(y_share * x_part, extent), tables)
            along, slope, deep = 0.0, 0.0, 0.0
            for y in range(y_share):
                rows_at = slice(y * x_part, (y + 1) * x_part)
                value, derivative = y_ref[0, index, pl.ds(y, 1)], y_ref[1, index, pl.ds(y, 1)]
                along = along + result[rows_at, :128] * value
                slope = slope + result[rows_at, :128] * derivative
                deep = deep + result[rows_at, 128:] * value
            value, derivative = xg_ref[x_window, at], xh_ref[x_window, at]
            terms = (derivative * along, value * slope, value * deep, value * along)
            return tuple(
                old + jnp.sum(term.reshape(-1, 8, 128), axis=0) for old, term in zip(sums, terms)
            )

        start = tuple(jnp.zeros((8, 128), F32) for _ in range(4))
        sums = lax.fori_loop(0, extent // x_part, over_x, start)
        for at_sum in range(4):
            total_row = jnp.sum(sums[at_sum], axis=0, keepdims=True)
            proj_ref[at_sum : at_sum + 1, at] = total_row * scale_ref[:, at]
        return carry

    lax.fori_loop(0, width // 128, project, 0)
    folded = jnp.zeros((4, live_total), F32)
    for k in range(len(kernel_weights)):
        folded = folded + proj_ref[:, k * live_total : (k + 1) * live_total]
    tile_ref[0:3] = (-force_unit * weight) * folded[0:3]
    embedding = weight * jnp.sum(folded[3:4], axis=1, keepdims=True) / cells
    line = jnp.zeros((1, live_total), F32)
    tile_lane = iota((1, live_total), 1)
    for at, value in enumerate(stress + [embedding]):
        line = jnp.where(tile_lane == at, value, line)
    tile_ref[3:4] = line
    tiles_ref[me] = tile_ref[...]
    start_tiles, wait_tiles = broadcast(1, tile_ref, tiles_ref)
    start_tiles()

    for chunk in range(chunks):
        own_back(chunk).wait()
    def force_to_atoms():
        wait_tiles(1, total)
        summed = tiles_ref[0]
        for source in range(1, total):
            summed = summed + tiles_ref[source]
        slot_lanes = (iota((live_total, 128), 0).astype(F32) - place_ref[0:1, 0:1]) == iota(
            (live_total, 128), 1
        ).astype(F32)
        slot_lanes = slot_lanes & (iota((live_total, 128), 1) < live)
        slot_force = jnp.dot(summed, slot_lanes.astype(F32), precision=HIGH, preferred_element_type=F32)
        near_column = jnp.full((128, 1), -1, jnp.int32)
        for slot in range(cap):
            near_column = jnp.where(iota((128, 1), 0) == slot, near_ref[slot], near_column)
        at_atom = (iota((128, atoms), 1) == near_column).astype(F32)
        atom_force = jnp.dot(slot_force, at_atom, precision=HIGH, preferred_element_type=F32)
        force_out[...] = atom_force[0:3]
        return summed

    def merged(parts):
        norm = sum(part[0] for part in parts)
        inner = sum(part[1] for part in parts)
        filled = norm > 0.0
        energy = jnp.where(filled, inner / jnp.where(filled, norm, 1.0), 0.0)
        square = 0.0
        for part_norm, part_inner, part_square in parts:
            filled = part_norm > 0.0
            part_energy = jnp.where(filled, part_inner / jnp.where(filled, part_norm, 1.0), 0.0)
            away = part_energy - energy
            square = square + part_square + away * away * part_norm
        return norm, inner, square

    def image_of(part, sums):
        for chunk in range(chunks):
            for step in range(1, gvec_size):
                back_copy(step, chunk, part).wait_recv()
        norm = jnp.zeros((8, extent), F32)
        inner = jnp.zeros((8, extent), F32)
        for pair in range(grain // 2):
            first = part * grain + 2 * pair
            both = jnp.concatenate(
                [
                    jnp.concatenate(
                        [
                            back_ref[source, chunk, first + side]
                            for source in range(gvec_size)
                            for chunk in range(chunks)
                        ],
                        axis=0,
                    )
                    for side in range(2)
                ],
                axis=1,
            )
            section = dot(cos_ref[1], both).astype(BF16)
            waves = dot(section, diag_ref[1])
            for side in range(2):
                a = first + side
                wide = coeff_ref[a].astype(F32)
                x_wave = x_wave_of(a)
                image = (0.5 * x_wave * x_wave + plane_kinetic) * wide
                image = image + waves[:, side * extent : (side + 1) * extent]
                image_ref[a] = image
                norm = norm + jnp.sum((wide * wide).reshape(-1, 8, extent), axis=0)
                inner = inner + jnp.sum((wide * image).reshape(-1, 8, extent), axis=0)
        norm, inner = total_of(norm), total_of(inner)
        filled = norm > 0.0
        energy = jnp.where(filled, inner / jnp.where(filled, norm, 1.0), 0.0)
        square = jnp.zeros((8, extent), F32)
        for side in range(grain):
            a = part * grain + side
            wide = coeff_ref[a].astype(F32)
            image = image_ref[a]
            residual = image - energy * wide
            square = square + jnp.sum((residual * residual).reshape(-1, 8, extent), axis=0)
            image_ref[a] = wide - image * recip_ref[a]
        return merged([sums, (norm, inner, total_of(square))])

    nothing = jnp.zeros((1, 1), F32)
    sums = lax.fori_loop(0, grains - 1, image_of, (nothing, nothing, nothing))
    summed = force_to_atoms()
    own = image_of(grains - 1, sums)
    for at, value in enumerate(own):
        last_ref[at : at + 1] = jnp.broadcast_to(value, (1, 128))
    lasts_ref[me] = last_ref[...]
    start_last, wait_last = broadcast(2, last_ref, lasts_ref)
    start_last()
    wait_last(1, gvec_size)
    parts = []
    for source in range(gvec_size):
        other = lasts_ref[(band_id * gvec_size + source) * dom_size + dom_id]
        parts.append(tuple(other[at : at + 1] for at in range(3)))
    norm, inner, square = merged(parts)
    energy = inner / norm

    def update(index, carry):
        for side in range(4):
            a = index * 4 + side
            wide = coeff_ref[a].astype(F32)
            waves_ref[0, a] = (image_ref[a] + energy * (wide * recip_ref[a])).astype(BF16)
        return carry

    lax.fori_loop(0, x_local // 4, update, 0)

    wait_last(gvec_size, total)
    band_sum = jnp.zeros((1, 128), F32)
    for band in range(band_size):
        for dom in range(dom_size):
            both = 0.0
            for source in range(gvec_size):
                both = both + lasts_ref[(band * gvec_size + source) * dom_size + dom]
            shifted = band * dom_size + dom - 0.5 * band_total
            occupied = float(2.0 / (1.0 + np.exp(shifted / (0.125 * band_total))))
            band_sum = band_sum + occupied * (both[1:2] / both[0:1])
    misc_lane = iota((1, 128), 1)
    misc_ref[0:1] = jnp.broadcast_to(energy, (1, 128))
    misc_ref[1:2] = jnp.broadcast_to(square / norm, (1, 128))
    misc_ref[2:3] = jnp.where(misc_lane == 7, band_sum / float(band_total), summed[3:4, :128])
    misc_ref[3:8] = jnp.zeros((5, 128), F32)

    for step in range(1, gvec_size):
        for part in range(ahead):
            lead_copy(step, part).wait_send()
        for chunk in range(chunks):
            forward_copy(step, chunk).wait_send()
            for part in range(grains):
                back_copy(step, chunk, part).wait_send()


def finish_kernel(parts, waves_ref, force_ref, misc_ref, waves_hbm, energy_ref, ratio_ref, force_out, total_ref, sems):
    size = waves_ref.shape[1] // parts
    copies = [
        pltpu.make_async_copy(
            waves_ref.at[:, pl.ds(part * size, size)], waves_hbm.at[:, pl.ds(part * size, size)], sems.at[part]
        )
        for part in range(parts)
    ]
    for copy in copies:
        copy.start()
    energy_ref[...] = misc_ref[0:1, 0:1]
    ratio_ref[...] = misc_ref[1:2, 0:1]
    total_ref[...] = misc_ref[2:3, 0:8]
    force_out[...] = force_ref[...]
    for copy in copies:
        copy.wait()


def per_device(sizes, coeffs, v_local, atom_pos, atom_charge, near_list, live_count):
    gvec_size = sizes[1]
    total = sizes[0] * sizes[1] * sizes[2]
    local_bands, x_local, extent, _ = coeffs.shape
    assert local_bands == 1
    y_share = v_local.shape[1]
    cap = near_list.shape[0]
    atoms = atom_pos.shape[1]
    live_total = total * cap // 4
    width = len(kernel_weights) * live_total
    y_chunk = 16 if y_share % 16 == 0 else y_share
    chunks = y_share // y_chunk
    piece = 16 if x_local % 16 == 0 else x_local
    pieces = x_local // piece
    grains = x_local // (8 if x_local % 8 == 0 else x_local)
    lanes = -(-(4 * cap + 1) // 128) * 128
    pair, diagonal = constant_tables(extent)
    groups = np.tril(np.ones((total, total), np.float32), -1)
    vmem = pl.BlockSpec(memory_space=pltpu.VMEM)
    smem = pl.BlockSpec(memory_space=pltpu.SMEM)
    hbm = pl.BlockSpec(memory_space=pltpu.HBM)
    plan = (x_local, extent, y_share, cap, live_total, atoms)
    deep = max(piece, y_chunk, 16)
    dma = pltpu.SemaphoreType.DMA
    operands = [
        pltpu.with_memory_space_constraint(operand, pltpu.HBM)
        for operand in (
            near_list, atom_pos, atom_charge.reshape(1, atoms), jnp.asarray(pair),
            jnp.asarray(diagonal), jnp.asarray(groups), coeffs, v_local,
        )
    ]
    waves_new, atom_force, misc = pl.pallas_call(
        functools.partial(step_kernel, sizes, plan),
        out_shape=(
            jax.ShapeDtypeStruct(coeffs.shape, BF16),
            jax.ShapeDtypeStruct((3, atoms), F32),
            jax.ShapeDtypeStruct((8, 128), F32),
        ),
        in_specs=[hbm, smem] + [hbm] * 7,
        out_specs=(vmem, vmem, vmem),
        scratch_shapes=[
            pltpu.SMEM(near_list.shape, jnp.int32),
            pltpu.VMEM(atom_pos.shape, F32),
            pltpu.VMEM((1, atoms), F32),
            pltpu.VMEM(pair.shape, BF16),
            pltpu.VMEM(diagonal.shape, BF16),
            pltpu.VMEM(groups.shape, F32),
            pltpu.VMEM((x_local, extent, extent), BF16),
            pltpu.VMEM(v_local.shape, BF16),
            pltpu.VMEM((deep * extent, extent), F32),
            pltpu.VMEM((extent, x_local, extent), BF16),
            pltpu.VMEM((gvec_size, y_share, x_local, extent), BF16),
            pltpu.VMEM((y_share, extent, extent), F32),
            pltpu.VMEM((y_share, extent, extent), BF16),
            pltpu.VMEM((chunks, extent, y_chunk, extent), BF16),
            pltpu.VMEM((gvec_size, chunks, x_local, y_chunk, extent), BF16),
            pltpu.VMEM((x_local, extent, extent), F32),
            pltpu.VMEM((x_local, extent, extent), F32),
            pltpu.VMEM((3, extent, extent), F32),
            pltpu.VMEM((1, lanes), F32),
            pltpu.VMEM((total, 1, lanes), F32),
            pltpu.VMEM((4, live_total), F32),
            pltpu.VMEM((total, 4, live_total), F32),
            pltpu.VMEM((3, 128), F32),
            pltpu.VMEM((total, 3, 128), F32),
            pltpu.VMEM((extent, width), F32),
            pltpu.VMEM((extent, width), F32),
            pltpu.VMEM((y_share, width), F32),
            pltpu.VMEM((2, width // 128, y_share, 128), F32),
            pltpu.VMEM((width, extent), BF16),
            pltpu.VMEM((extent, width), BF16),
            pltpu.VMEM((extent, width), BF16),
            pltpu.VMEM((1, width), F32),
            pltpu.VMEM((8, 128), F32),
            pltpu.VMEM((4, width), F32),
            dma((pieces,)),
            dma,
            dma((6,)),
            dma((1 + chunks,)),
            dma((gvec_size, chunks + pieces // 2)),
            dma((gvec_size, chunks + pieces // 2)),
            dma((gvec_size, chunks, grains)),
            dma((gvec_size, chunks, grains)),
            dma((3, total)),
            dma((3, total)),
        ],
        compiler_params=pltpu.CompilerParams(
            collective_id=0, has_side_effects=True, vmem_limit_bytes=36 * 1024 * 1024
        ),
        name="step",
    )(operands[0], live_count, *operands[1:])
    parts = 4 if x_local % 4 == 0 else 1
    scalar = jax.ShapeDtypeStruct((1, 1), F32)
    waves_new, energy, ratio, atom_force, totals = pl.pallas_call(
        functools.partial(finish_kernel, parts),
        out_shape=(
            jax.ShapeDtypeStruct(coeffs.shape, BF16), scalar, scalar,
            jax.ShapeDtypeStruct((3, atoms), F32), jax.ShapeDtypeStruct((1, 8), F32),
        ),
        in_specs=[vmem] * 3,
        out_specs=(hbm, vmem, vmem, vmem, vmem),
        scratch_shapes=[dma((parts,))],
        compiler_params=pltpu.CompilerParams(vmem_limit_bytes=8 * 1024 * 1024),
        name="finish",
    )(waves_new, atom_force, misc)
    return (waves_new, energy.reshape(1), ratio.reshape(1), atom_force, totals.reshape(8))


def solution(mesh):
    sizes = (mesh.shape["band"], mesh.shape["gvec"], mesh.shape["dom"])
    return jax.shard_map(
        functools.partial(per_device, sizes),
        mesh=mesh,
        in_specs=(
            P(("band", "dom"), "gvec", None, None),
            P(None, "gvec", None),
            P(None, ("band", "gvec", "dom")),
            P(("band", "gvec", "dom")),
            P(("band", "gvec", "dom")),
            P(("band", "gvec", "dom")),
        ),
        out_specs=(
            P(("band", "dom"), "gvec", None, None),
            P(("band", "dom")),
            P(("band", "dom")),
            P(None, ("band", "gvec", "dom")),
            P(),
        ),
        check_vma=False,
    )
```

```python
import functools

import jax
import jax.numpy as jnp
import numpy as np
from jax import lax
from jax.experimental import pallas as pl
from jax.experimental.pallas import tpu as pltpu
from jax.sharding import PartitionSpec as P

sigma_fractions = (1.0 / 32.0, 1.0 / 16.0, 1.0 / 8.0, 1.0 / 4.0)
kernel_weights = (1.0, 0.5, 0.25, 0.125)
force_unit = 1.0 / 4096.0
step_size = 0.5
MESH = pl.DeviceIdType.MESH
F32 = jnp.float32
BF16 = jnp.bfloat16
HIGH = lax.Precision.HIGHEST


def cosine_table(length):
    points = np.arange(length).astype(np.float32)
    angles = np.float32(np.pi) * (points[:, None] + np.float32(0.5)) * points[None, :] / np.float32(length)
    scales = np.where(points == 0.0, np.sqrt(1.0 / length), np.sqrt(2.0 / length)).astype(np.float32)
    return (np.cos(angles.astype(np.float64)).astype(np.float32) * scales[None, :]).astype(jnp.bfloat16)


def constant_tables(length):
    cosines = cosine_table(length)
    zero = np.zeros_like(cosines)
    pair = np.stack([cosines, cosines.T])
    diagonal = np.stack(
        [np.block([[cosines.T, zero], [zero, cosines.T]]), np.block([[cosines, zero], [zero, cosines]])]
    )
    return pair, diagonal


def dot(left, right):
    return jnp.dot(left, right, preferred_element_type=F32)


def total_of(value):
    return jnp.sum(jnp.sum(value, axis=0, keepdims=True), axis=1, keepdims=True)


def iota(shape, axis):
    return lax.broadcasted_iota(jnp.int32, shape, axis)


def step_kernel(
    sizes, plan,
    near_hbm, live_ref, pos_hbm, charge_hbm, cos_hbm, diag_hbm, group_hbm, coeff_hbm, local_hbm,
    waves_ref, force_out, misc_ref,
    near_ref, pos_ref, charge_ref, cos_ref, diag_ref, group_ref, coeff_ref, local_ref, stage_ref, sect_ref,
    held_ref, field_ref, dens_ref, going_ref, back_ref, recip_ref, moment_ref, row_ref, rows_ref,
    tile_ref, gvec_tiles, band_tiles, dom_tiles, pair_ref, pairs_ref, square_ref, squares_ref,
    xg_ref, xh_ref, yg_ref, y_ref, depth_ref, zg_ref, zh_ref, scale_ref, place_ref, proj_ref,
    load_sem, local_sem, small_sem, own_sem, fsend, frecv, bsend, brecv, csend, crecv,
):
    band_size, gvec_size, dom_size = sizes
    total = band_size * gvec_size * dom_size
    x_local, extent, y_share, cap, live_total, atoms = plan
    band_id, gvec_id, dom_id = lax.axis_index("band"), lax.axis_index("gvec"), lax.axis_index("dom")
    me = (dom_id * band_size + band_id) * gvec_size + gvec_id
    band_total = band_size * dom_size
    width = len(kernel_weights) * live_total
    cells = float(extent**3)
    wave_step = np.float32(np.pi / extent)
    y_chunk = 16 if y_share % 16 == 0 else y_share
    chunks = y_share // y_chunk
    piece = 16 if x_local % 16 == 0 else x_local
    pieces = x_local // piece
    grain = 8 if x_local % 8 == 0 else x_local
    grains = x_local // grain
    early = max(chunks - 2, 0)
    barrier = pltpu.get_barrier_semaphore()

    def load_of(part):
        window = pl.ds(part * piece, piece)
        return pltpu.make_async_copy(coeff_hbm.at[0, window], coeff_ref.at[window], load_sem.at[part])

    smalls = [
        pltpu.make_async_copy(source, target, small_sem.at[at])
        for at, (source, target) in enumerate(
            (
                (near_hbm, near_ref), (pos_hbm, pos_ref), (charge_hbm, charge_ref),
                (cos_hbm, cos_ref), (diag_hbm, diag_ref), (group_hbm, group_ref),
            )
        )
    ]
    for copy in smalls:
        copy.start()
    for part in range(pieces):
        load_of(part).start()
    local_copy = pltpu.make_async_copy(local_hbm, local_ref, local_sem)
    local_copy.start()

    band_at = [lax.rem(band_id + shift, band_size) for shift in range(band_size)]
    gvec_at = [lax.rem(gvec_id + shift, gvec_size) for shift in range(gvec_size)]
    dom_at = [lax.rem(dom_id + shift, dom_size) for shift in range(dom_size)]

    axis_peers = (
        [(band_id, gvec_at[step], dom_id) for step in range(gvec_size)],
        [(band_at[step], gvec_id, dom_id) for step in range(band_size)],
        [(band_id, gvec_id, dom_at[step]) for step in range(dom_size)],
    )
    for peers in axis_peers:
        for peer in peers[1:]:
            pl.semaphore_signal(barrier, inc=1, device_id=peer, device_id_type=MESH)

    def exchange(kind, axis, src, dst):
        return [
            pltpu.make_async_remote_copy(
                src_ref=src, dst_ref=dst,
                send_sem=csend.at[kind, axis, step], recv_sem=crecv.at[kind, axis, step],
                device_id=axis_peers[axis][step], device_id_type=MESH,
            )
            for step in range(1, len(axis_peers[axis]))
        ]

    def start_all(copies):
        for copy in copies:
            copy.start()
        return copies

    def wait_all(copies):
        for copy in copies:
            copy.wait()

    group = piece
    smalls[3].wait()
    smalls[4].wait()

    def forward(index, carry):
        load_of(index).wait()
        for pair in range(group // 2):
            first = index * group + 2 * pair
            both = jnp.concatenate([coeff_ref[first], coeff_ref[first + 1]], axis=1)
            section = dot(both, diag_ref[0]).astype(BF16)
            result = dot(cos_ref[0], section)
            stage_ref[pl.ds(2 * pair * extent, extent)] = result[:, :extent]
            stage_ref[pl.ds((2 * pair + 1) * extent, extent)] = result[:, extent:]
        window = pl.ds(pl.multiple_of(index * group, group), group)

        def spread(outer, inner_carry):
            for inner in range(8):
                y = outer * 8 + inner
                sect_ref[y, window] = stage_ref[pl.ds(y, group, stride=extent)].astype(BF16)
            return inner_carry

        lax.fori_loop(0, extent // 8, spread, 0)
        return carry

    ahead = pieces // 2

    def gvec_peer(step):
        return (band_id, gvec_at[step], dom_id)

    def lead_copy(step, part):
        window = pl.ds(part * piece, piece)
        return pltpu.make_async_remote_copy(
            src_ref=sect_ref.at[pl.ds(gvec_at[step] * y_share, y_share), window],
            dst_ref=held_ref.at[gvec_id, :, window],
            send_sem=fsend.at[step, chunks + part], recv_sem=frecv.at[step, chunks + part],
            device_id=gvec_peer(step), device_id_type=MESH,
        )

    def forward_copy(step, chunk):
        owner = gvec_at[step]
        window = pl.ds(ahead * piece, x_local - ahead * piece)
        return pltpu.make_async_remote_copy(
            src_ref=sect_ref.at[pl.ds(owner * y_share + chunk * y_chunk, y_chunk), window],
            dst_ref=held_ref.at[gvec_id, pl.ds(chunk * y_chunk, y_chunk), window],
            send_sem=fsend.at[step, chunk], recv_sem=frecv.at[step, chunk],
            device_id=gvec_peer(step), device_id_type=MESH,
        )

    if ahead:
        forward(0, 0)
    pl.semaphore_wait(barrier, band_size + gvec_size + dom_size - 3)
    if ahead:
        for step in range(1, gvec_size):
            lead_copy(step, 0).start()

    for at in (0, 1, 2, 5):
        smalls[at].wait()

    lanes = row_ref.shape[1]
    lane = iota((1, lanes), 1)
    near_row = jnp.full((1, lanes), -1, jnp.int32)
    for quantity in range(4):
        for slot in range(cap):
            near_row = jnp.where(lane == quantity * cap + slot, near_ref[slot], near_row)
    live = live_ref[0]
    chosen = (iota((atoms, lanes), 0) == near_row).astype(F32)
    picked_pos = jnp.dot(pos_ref[...], chosen, precision=HIGH, preferred_element_type=F32)
    picked_charge = jnp.dot(charge_ref[...], chosen, precision=HIGH, preferred_element_type=F32)
    row = jnp.zeros((1, lanes), F32)
    for quantity in range(3):
        part = (lane >= quantity * cap) & (lane < (quantity + 1) * cap)
        row = jnp.where(part, picked_pos[quantity : quantity + 1], row)
    part = (lane >= 3 * cap) & (lane < 3 * cap + live) & (lane < 4 * cap)
    row = jnp.where(part, picked_charge, row)
    row = jnp.where(lane == 4 * cap, live.astype(F32), row)
    row_ref[...] = row
    rows_ref[dom_id, band_id, gvec_id] = row
    copies = start_all(exchange(0, 0, row_ref, rows_ref.at[dom_id, band_id, gvec_id]))

    def lead(part, carry):
        forward(part, carry)
        for step in range(1, gvec_size):
            lead_copy(step, part).start()
        return carry

    lax.fori_loop(1, ahead, lead, 0)
    wait_all(copies)
    copies = start_all(exchange(0, 1, rows_ref.at[dom_id, band_id], rows_ref.at[dom_id, band_id]))
    lax.fori_loop(ahead, pieces, forward, 0)
    for chunk in range(chunks):
        for step in range(1, gvec_size):
            forward_copy(step, chunk).start()
    own_copy = pltpu.make_async_copy(
        sect_ref.at[pl.ds(gvec_id * y_share, y_share)], held_ref.at[gvec_id], own_sem.at[0]
    )
    own_copy.start()
    wait_all(copies)
    copies = start_all(exchange(0, 2, rows_ref.at[dom_id], rows_ref.at[dom_id]))

    local_copy.wait()
    x_block = 16

    def turn_local(index, carry):
        window = pl.ds(pl.multiple_of(index * x_block, x_block), x_block)
        stage_ref[pl.ds(0, x_block * y_share)] = (
            local_ref[window].astype(F32).reshape(x_block * y_share, extent)
        )

        def turn(outer, inner_carry):
            for inner in range(8):
                y = outer * 8 + inner
                field_ref[y, window] = stage_ref[pl.ds(y, x_block, stride=y_share)]
            return inner_carry

        lax.fori_loop(0, y_share // 8, turn, 0)
        return carry

    lax.fori_loop(0, extent // x_block, turn_local, 0)

    wait_all(copies)
    rows = rows_ref[...].reshape(total, row_ref.shape[1])
    count = rows[:, 4 * cap : 4 * cap + 1]
    count_wide = jnp.broadcast_to(count, (total, live_total))
    offset = jnp.dot(group_ref[...], count_wide, precision=HIGH, preferred_element_type=F32)
    order = iota((total, live_total), 1).astype(F32)
    holds = ((order >= offset) & (order < offset + count_wide)).astype(F32)
    slot_at = jnp.sum(holds * (order - offset), axis=0, keepdims=True)
    spread_rows = lax.dot_general(
        rows, holds, (((0,), (0,)), ((), ())), precision=HIGH, preferred_element_type=F32
    )
    here = (iota((cap, live_total), 0).astype(F32) == slot_at).astype(F32)
    centre = [
        jnp.sum(spread_rows[k * cap : (k + 1) * cap] * here, axis=0, keepdims=True) for k in range(4)
    ]
    mine = (iota((total, 1), 0) == me).astype(F32)
    own_offset = jnp.sum(mine * offset[:, :1], axis=0, keepdims=True)
    place_ref[...] = jnp.broadcast_to(own_offset, place_ref.shape)

    x_points = iota((extent, live_total), 0).astype(F32)
    y_points = (iota((y_share, live_total), 0) + gvec_id * y_share).astype(F32)
    for k, fraction in enumerate(sigma_fractions):
        exponent = 0.5 / (extent * fraction) ** 2
        window = slice(k * live_total, (k + 1) * live_total)
        scaled = kernel_weights[k] * centre[3]
        scale_ref[:, window] = scaled
        away = x_points - centre[0]
        value = jnp.exp(-exponent * away * away)
        xg_ref[:, window] = value
        xh_ref[:, window] = 2.0 * exponent * away * value
        away = y_points - centre[1]
        value = jnp.exp(-exponent * away * away)
        slope = 2.0 * exponent * away * value
        yg_ref[:, window] = value
        for part in range(live_total // 128):
            y_ref[0, k * live_total // 128 + part] = value[:, part * 128 : (part + 1) * 128]
            y_ref[1, k * live_total // 128 + part] = slope[:, part * 128 : (part + 1) * 128]
        away = x_points - centre[2]
        value = jnp.exp(-exponent * away * away)
        depth_ref[window] = jnp.transpose(scaled * value).astype(BF16)
        zg_ref[:, window] = value.astype(BF16)
        zh_ref[:, window] = (2.0 * exponent * away * value).astype(BF16)

    block = min(width, 512)

    field_rows = 4

    def add_field(index, carry):
        value = None
        for part in range(width // block):
            window = slice(part * block, (part + 1) * block)
            plane = jnp.concatenate(
                [
                    (xg_ref[:, window] * yg_ref[pl.ds(index * field_rows + side, 1), window]).astype(BF16)
                    for side in range(field_rows)
                ],
                axis=0,
            )
            term = dot(plane, depth_ref[window])
            value = term if value is None else value + term
        value = value.astype(BF16).astype(F32)
        for side in range(field_rows):
            field_ref[index * field_rows + side] += value[side * extent : (side + 1) * extent]
        return carry

    lax.fori_loop(0, y_share // field_rows, add_field, 0)

    def back_copy(step, chunk, part):
        owner = gvec_at[step]
        return pltpu.make_async_remote_copy(
            src_ref=going_ref.at[chunk, pl.ds(owner * x_local + part * grain, grain)],
            dst_ref=back_ref.at[gvec_id, chunk, pl.ds(part * grain, grain)],
            send_sem=bsend.at[step, chunk, part], recv_sem=brecv.at[step, chunk, part],
            device_id=gvec_peer(step), device_id_type=MESH,
        )

    def early_copy(step, chunk):
        return pltpu.make_async_remote_copy(
            src_ref=going_ref.at[chunk, pl.ds(gvec_at[step] * x_local, x_local)],
            dst_ref=back_ref.at[gvec_id, chunk],
            send_sem=bsend.at[step, chunk, 0], recv_sem=brecv.at[step, chunk, 0],
            device_id=gvec_peer(step), device_id_type=MESH,
        )

    def own_back(chunk):
        return pltpu.make_async_copy(
            going_ref.at[chunk, pl.ds(gvec_id * x_local, x_local)],
            back_ref.at[gvec_id, chunk], own_sem.at[1 + chunk],
        )

    own_copy.wait()

    for step in range(1, gvec_size):
        for part in range(ahead):
            lead_copy(step, part).wait_recv()

    def middle(chunk, inner):
        for step in range(1, gvec_size):
            forward_copy(step, chunk).wait_recv()
        for pair in range(y_chunk // 2):
            first = chunk * y_chunk + 2 * pair
            both = jnp.concatenate(
                [
                    jnp.concatenate([held_ref[source, first + side] for source in range(gvec_size)], axis=0)
                    for side in range(2)
                ],
                axis=1,
            )
            wide = dot(cos_ref[0], both).astype(BF16).astype(F32)
            square = (wide * wide).astype(BF16)
            dens_ref[first] = square[:, :extent]
            dens_ref[first + 1] = square[:, extent:]
            fields = jnp.concatenate([field_ref[first], field_ref[first + 1]], axis=1)
            applied = (fields * wide).astype(BF16)
            result = dot(cos_ref[1], applied)
            stage_ref[pl.ds(2 * pair * extent, extent)] = result[:, :extent]
            stage_ref[pl.ds((2 * pair + 1) * extent, extent)] = result[:, extent:]
            inner = inner + jnp.sum((applied.astype(F32) * wide).reshape(-1, 8, 2 * extent), axis=0)

        def spread(outer, inner_carry):
            for side in range(8):
                a = outer * 8 + side
                going_ref[chunk, a] = stage_ref[pl.ds(a, y_chunk, stride=extent)].astype(BF16)
            return inner_carry

        lax.fori_loop(0, extent // 8, spread, 0)
        own_back(chunk).start()
        return inner

    def middle_early(chunk, inner):
        inner = middle(chunk, inner)
        for step in range(1, gvec_size):
            early_copy(step, chunk).start()
        return inner

    inner = lax.fori_loop(0, early, middle_early, jnp.zeros((8, 2 * extent), F32))
    inner = lax.fori_loop(early, chunks, middle, inner)

    def send_late(part, carry):
        for chunk in range(early, chunks):
            for step in range(1, gvec_size):
                back_copy(step, chunk, part).start()
        return carry

    lax.fori_loop(0, grains, send_late, 0)

    q_wave = iota((extent, extent), 0).astype(F32) * wave_step
    l_wave = iota((extent, extent), 1).astype(F32) * wave_step
    plane_kinetic = 0.5 * (q_wave * q_wave + l_wave * l_wave)
    moment_ref[...] = jnp.zeros_like(moment_ref)

    def x_wave_of(a):
        return jnp.full((1, 1), gvec_id * x_local + a, jnp.int32).astype(F32) * wave_step

    def coefficients(index, carry):
        zero, one, two = 0.0, 0.0, 0.0
        for inner in range(4):
            a = index * 4 + inner
            wide = coeff_ref[a].astype(F32)
            x_wave = x_wave_of(a)
            square = wide * wide
            by_x = square * x_wave
            zero, one, two = zero + square, one + by_x, two + by_x * x_wave
            recip_ref[a] = step_size / (1.0 + 0.5 * x_wave * x_wave + plane_kinetic)
        moment_ref[0] += zero
        moment_ref[1] += one
        moment_ref[2] += two
        return carry

    lax.fori_loop(0, x_local // 4, coefficients, 0)
    group_id = band_id * dom_size + dom_id
    shifted = jnp.full((1, 1), group_id, jnp.int32).astype(F32) - 0.5 * band_total
    weight = 2.0 / (1.0 + jnp.exp(shifted / (0.125 * band_total)))
    terms = (
        moment_ref[2],
        moment_ref[0] * q_wave * q_wave,
        moment_ref[0] * l_wave * l_wave,
        moment_ref[1] * q_wave,
        moment_ref[1] * l_wave,
        moment_ref[0] * q_wave * l_wave,
    )
    terms = [total_of(term) for term in terms]
    stress = [weight * term / cells for term in terms]
    norm = total_of(moment_ref[0])
    inner = total_of(inner) + 0.5 * (terms[0] + terms[1] + terms[2])
    pair_ref[0:1] = jnp.broadcast_to(norm, (1, 128))
    pair_ref[1:2] = jnp.broadcast_to(inner, (1, 128))
    pairs_ref[gvec_id] = pair_ref[...]
    pair_copies = start_all(exchange(2, 0, pair_ref, pairs_ref.at[gvec_id]))

    x_part = 32

    def project(index, carry):
        at = pl.ds(pl.multiple_of(index * 128, 128), 128)
        tables = jnp.concatenate([zg_ref[:, at], zh_ref[:, at]], axis=1)

        def over_x(x_at, sums):
            x_window = pl.ds(pl.multiple_of(x_at * x_part, x_part), x_part)
            result = dot(dens_ref[:, x_window].reshape(y_share * x_part, extent), tables)
            along, slope, deep = 0.0, 0.0, 0.0
            for y in range(y_share):
                rows_at = slice(y * x_part, (y + 1) * x_part)
                value, derivative = y_ref[0, index, pl.ds(y, 1)], y_ref[1, index, pl.ds(y, 1)]
                along = along + result[rows_at, :128] * value
                slope = slope + result[rows_at, :128] * derivative
                deep = deep + result[rows_at, 128:] * value
            value, derivative = xg_ref[x_window, at], xh_ref[x_window, at]
            terms = (derivative * along, value * slope, value * deep, value * along)
            return tuple(
                old + jnp.sum(term.reshape(-1, 8, 128), axis=0) for old, term in zip(sums, terms)
            )

        start = tuple(jnp.zeros((8, 128), F32) for _ in range(4))
        sums = lax.fori_loop(0, extent // x_part, over_x, start)
        for at_sum in range(4):
            total_row = jnp.sum(sums[at_sum], axis=0, keepdims=True)
            proj_ref[at_sum : at_sum + 1, at] = total_row * scale_ref[:, at]
        return carry

    lax.fori_loop(0, width // 128, project, 0)
    folded = jnp.zeros((4, live_total), F32)
    for k in range(len(kernel_weights)):
        folded = folded + proj_ref[:, k * live_total : (k + 1) * live_total]
    tile_ref[0:3] = (-force_unit * weight) * folded[0:3]
    embedding = weight * jnp.sum(folded[3:4], axis=1, keepdims=True) / cells
    line = jnp.zeros((1, live_total), F32)
    tile_lane = iota((1, live_total), 1)
    wait_all(pair_copies)
    both = sum(pairs_ref[source] for source in range(gvec_size))
    norm, inner = both[0:1], both[1:2]
    energy = inner / norm
    misc_ref[0:1] = energy
    band_energy = weight * energy[:, 0:1] / float(gvec_size * band_total)
    for at, value in enumerate(stress + [embedding, band_energy]):
        line = jnp.where(tile_lane == at, value, line)
    tile_ref[3:4] = line

    def tile_stage(axis, slots, at):
        slots[at] = tile_ref[...]
        return start_all(exchange(1, axis, tile_ref, slots.at[at]))

    def tile_sum(copies, slots):
        wait_all(copies)
        value = slots[0]
        for source in range(1, slots.shape[0]):
            value = value + slots[source]
        tile_ref[...] = value

    copies = tile_stage(0, gvec_tiles, gvec_id)

    for chunk in range(chunks):
        own_back(chunk).wait()
    for chunk in range(early):
        for step in range(1, gvec_size):
            early_copy(step, chunk).wait_recv()

    def image_of(part, square):
        for chunk in range(early, chunks):
            for step in range(1, gvec_size):
                back_copy(step, chunk, part).wait_recv()
        for pair in range(grain // 2):
            first = part * grain + 2 * pair
            both = jnp.concatenate(
                [
                    jnp.concatenate(
                        [
                            back_ref[source, chunk, first + side]
                            for source in range(gvec_size)
                            for chunk in range(chunks)
                        ],
                        axis=0,
                    )
                    for side in range(2)
                ],
                axis=1,
            )
            section = dot(cos_ref[1], both).astype(BF16)
            waves = dot(section, diag_ref[1])
            for side in range(2):
                a = first + side
                wide = coeff_ref[a].astype(F32)
                x_wave = x_wave_of(a)
                image = (0.5 * x_wave * x_wave + plane_kinetic) * wide
                image = image + waves[:, side * extent : (side + 1) * extent]
                residual = image - energy * wide
                square = square + jnp.sum((residual * residual).reshape(-1, 8, extent), axis=0)
                waves_ref[0, a] = (wide - residual * recip_ref[a]).astype(BF16)
        return square

    cuts = [(grains - 1) * at // 3 for at in range(4)]
    square = lax.fori_loop(cuts[0], cuts[1], image_of, jnp.zeros((8, extent), F32))
    tile_sum(copies, gvec_tiles)
    copies = tile_stage(1, band_tiles, band_id)
    square = lax.fori_loop(cuts[1], cuts[2], image_of, square)
    tile_sum(copies, band_tiles)
    copies = tile_stage(2, dom_tiles, dom_id)
    square = lax.fori_loop(cuts[2], cuts[3], image_of, square)
    tile_sum(copies, dom_tiles)

    summed = tile_ref[...]
    slot_lanes = (iota((live_total, 128), 0).astype(F32) - place_ref[0:1, 0:1]) == iota(
        (live_total, 128), 1
    ).astype(F32)
    slot_lanes = slot_lanes & (iota((live_total, 128), 1) < live)
    slot_force = jnp.dot(summed, slot_lanes.astype(F32), precision=HIGH, preferred_element_type=F32)
    near_column = jnp.full((128, 1), -1, jnp.int32)
    for slot in range(cap):
        near_column = jnp.where(iota((128, 1), 0) == slot, near_ref[slot], near_column)
    at_atom = (iota((128, atoms), 1) == near_column).astype(F32)
    atom_force = jnp.dot(slot_force, at_atom, precision=HIGH, preferred_element_type=F32)
    force_out[...] = atom_force[0:3]
    misc_ref[2:3] = summed[3:4, 0:128]
    misc_ref[3:8] = jnp.zeros((5, 128), F32)

    square = image_of(grains - 1, square)
    square_ref[...] = jnp.broadcast_to(total_of(square), (1, 128))
    squares_ref[gvec_id] = square_ref[...]
    wait_all(start_all(exchange(3, 0, square_ref, squares_ref.at[gvec_id])))
    square = sum(squares_ref[source] for source in range(gvec_size))
    misc_ref[1:2] = square / norm

    for step in range(1, gvec_size):
        for part in range(ahead):
            lead_copy(step, part).wait_send()
        for chunk in range(chunks):
            forward_copy(step, chunk).wait_send()
        for chunk in range(early):
            early_copy(step, chunk).wait_send()
        for chunk in range(early, chunks):
            for part in range(grains):
                back_copy(step, chunk, part).wait_send()


def finish_kernel(
    parts, waves_ref, force_ref, misc_ref,
    waves_hbm, force_hbm, energy_hbm, ratio_hbm, total_hbm, energy_ref, ratio_ref, total_ref, sems,
):
    size = waves_ref.shape[1] // parts
    pairs = [
        (waves_ref.at[:, pl.ds(part * size, size)], waves_hbm.at[:, pl.ds(part * size, size)])
        for part in range(parts)
    ]
    pairs += [
        (force_ref, force_hbm), (energy_ref, energy_hbm), (ratio_ref, ratio_hbm), (total_ref, total_hbm)
    ]
    copies = [
        pltpu.make_async_copy(source, target, sems.at[at]) for at, (source, target) in enumerate(pairs)
    ]
    for copy in copies[: parts + 1]:
        copy.start()
    energy_ref[...] = misc_ref[0:1, 0:1]
    ratio_ref[...] = misc_ref[1:2, 0:1]
    total_ref[...] = misc_ref[2:3, 0:8]
    for copy in copies[parts + 1 :]:
        copy.start()
    for copy in copies:
        copy.wait()


def per_device(sizes, coeffs, v_local, atom_pos, atom_charge, near_list, live_count):
    band_size, gvec_size, dom_size = sizes
    total = sizes[0] * sizes[1] * sizes[2]
    local_bands, x_local, extent, _ = coeffs.shape
    assert local_bands == 1
    y_share = v_local.shape[1]
    cap = near_list.shape[0]
    atoms = atom_pos.shape[1]
    live_total = total * cap // 4
    width = len(kernel_weights) * live_total
    y_chunk = 16 if y_share % 16 == 0 else y_share
    chunks = y_share // y_chunk
    piece = 16 if x_local % 16 == 0 else x_local
    pieces = x_local // piece
    grains = x_local // (8 if x_local % 8 == 0 else x_local)
    lanes = -(-(4 * cap + 1) // 128) * 128
    pair, diagonal = constant_tables(extent)
    groups = np.tril(np.ones((total, total), np.float32), -1)
    vmem = pl.BlockSpec(memory_space=pltpu.VMEM)
    smem = pl.BlockSpec(memory_space=pltpu.SMEM)
    hbm = pl.BlockSpec(memory_space=pltpu.HBM)
    plan = (x_local, extent, y_share, cap, live_total, atoms)
    deep = max(piece, y_chunk, 16)
    dma = pltpu.SemaphoreType.DMA
    operands = [
        pltpu.with_memory_space_constraint(operand, pltpu.HBM)
        for operand in (
            near_list, atom_pos, atom_charge.reshape(1, atoms), jnp.asarray(pair),
            jnp.asarray(diagonal), jnp.asarray(groups), coeffs, v_local,
        )
    ]
    scalar = jax.ShapeDtypeStruct((1, 1), F32)
    outs = (
        jax.ShapeDtypeStruct(coeffs.shape, BF16), jax.ShapeDtypeStruct((3, atoms), F32),
        scalar, scalar, jax.ShapeDtypeStruct((1, 8), F32),
    )
    results = pl.pallas_call(
        functools.partial(step_kernel, sizes, plan),
        out_shape=(outs[0], outs[1], jax.ShapeDtypeStruct((8, 128), F32)),
        in_specs=[hbm, smem] + [hbm] * 7,
        out_specs=(vmem,) * 3,
        scratch_shapes=[
            pltpu.SMEM(near_list.shape, jnp.int32),
            pltpu.VMEM(atom_pos.shape, F32),
            pltpu.VMEM((1, atoms), F32),
            pltpu.VMEM(pair.shape, BF16),
            pltpu.VMEM(diagonal.shape, BF16),
            pltpu.VMEM(groups.shape, F32),
            pltpu.VMEM((x_local, extent, extent), BF16),
            pltpu.VMEM(v_local.shape, BF16),
            pltpu.VMEM((deep * extent, extent), F32),
            pltpu.VMEM((extent, x_local, extent), BF16),
            pltpu.VMEM((gvec_size, y_share, x_local, extent), BF16),
            pltpu.VMEM((y_share, extent, extent), F32),
            pltpu.VMEM((y_share, extent, extent), BF16),
            pltpu.VMEM((chunks, extent, y_chunk, extent), BF16),
            pltpu.VMEM((gvec_size, chunks, x_local, y_chunk, extent), BF16),
            pltpu.VMEM((x_local, extent, extent), F32),
            pltpu.VMEM((3, extent, extent), F32),
            pltpu.VMEM((1, lanes), F32),
            pltpu.VMEM((dom_size, band_size, gvec_size, 1, lanes), F32),
            pltpu.VMEM((4, live_total), F32),
            pltpu.VMEM((gvec_size, 4, live_total), F32),
            pltpu.VMEM((band_size, 4, live_total), F32),
            pltpu.VMEM((dom_size, 4, live_total), F32),
            pltpu.VMEM((2, 128), F32),
            pltpu.VMEM((gvec_size, 2, 128), F32),
            pltpu.VMEM((1, 128), F32),
            pltpu.VMEM((gvec_size, 1, 128), F32),
            pltpu.VMEM((extent, width), F32),
            pltpu.VMEM((extent, width), F32),
            pltpu.VMEM((y_share, width), F32),
            pltpu.VMEM((2, width // 128, y_share, 128), F32),
            pltpu.VMEM((width, extent), BF16),
            pltpu.VMEM((extent, width), BF16),
            pltpu.VMEM((extent, width), BF16),
            pltpu.VMEM((1, width), F32),
            pltpu.VMEM((8, 128), F32),
            pltpu.VMEM((4, width), F32),
            dma((pieces,)),
            dma,
            dma((6,)),
            dma((1 + chunks,)),
            dma((gvec_size, chunks + pieces // 2)),
            dma((gvec_size, chunks + pieces // 2)),
            dma((gvec_size, chunks, grains)),
            dma((gvec_size, chunks, grains)),
            dma((4, 3, max(sizes))),
            dma((4, 3, max(sizes))),
        ],
        compiler_params=pltpu.CompilerParams(
            collective_id=0, has_side_effects=True, vmem_limit_bytes=36 * 1024 * 1024
        ),
        name="step",
    )(operands[0], live_count, *operands[1:])
    parts = 4 if x_local % 4 == 0 else 1
    waves_new, atom_force, energy, ratio, totals = pl.pallas_call(
        functools.partial(finish_kernel, parts),
        out_shape=outs,
        in_specs=[vmem] * 3,
        out_specs=(hbm,) * 5,
        scratch_shapes=[
            pltpu.VMEM((1, 1), F32), pltpu.VMEM((1, 1), F32), pltpu.VMEM((1, 8), F32), dma((parts + 4,)),
        ],
        compiler_params=pltpu.CompilerParams(vmem_limit_bytes=8 * 1024 * 1024),
        name="finish",
    )(*results)
    return (waves_new, energy.reshape(1), ratio.reshape(1), atom_force, totals.reshape(8))


def solution(mesh):
    sizes = (mesh.shape["band"], mesh.shape["gvec"], mesh.shape["dom"])
    return jax.shard_map(
        functools.partial(per_device, sizes),
        mesh=mesh,
        in_specs=(
            P(("band", "dom"), "gvec", None, None),
            P(None, "gvec", None),
            P(None, ("band", "gvec", "dom")),
            P(("band", "gvec", "dom")),
            P(("band", "gvec", "dom")),
            P(("band", "gvec", "dom")),
        ),
        out_specs=(
            P(("band", "dom"), "gvec", None, None),
            P(("band", "dom")),
            P(("band", "dom")),
            P(None, ("band", "gvec", "dom")),
            P(),
        ),
        check_vma=False,
    )
```

```python
import functools

import jax
import jax.numpy as jnp
import numpy as np
from jax import lax
from jax.experimental import pallas as pl
from jax.experimental.pallas import tpu as pltpu
from jax.sharding import PartitionSpec as P

sigma_fractions = (1.0 / 32.0, 1.0 / 16.0, 1.0 / 8.0, 1.0 / 4.0)
kernel_weights = (1.0, 0.5, 0.25, 0.125)
force_unit = 1.0 / 4096.0
step_size = 0.5
MESH = pl.DeviceIdType.MESH
F32 = jnp.float32
BF16 = jnp.bfloat16
HIGH = lax.Precision.HIGHEST


def cosine_table(length):
    points = np.arange(length).astype(np.float32)
    angles = np.float32(np.pi) * (points[:, None] + np.float32(0.5)) * points[None, :] / np.float32(length)
    scales = np.where(points == 0.0, np.sqrt(1.0 / length), np.sqrt(2.0 / length)).astype(np.float32)
    return (np.cos(angles.astype(np.float64)).astype(np.float32) * scales[None, :]).astype(jnp.bfloat16)


def constant_tables(length):
    cosines = cosine_table(length)
    zero = np.zeros_like(cosines)
    pair = np.stack([cosines, cosines.T])
    diagonal = np.stack(
        [np.block([[cosines.T, zero], [zero, cosines.T]]), np.block([[cosines, zero], [zero, cosines]])]
    )
    return pair, diagonal


def dot(left, right):
    return jnp.dot(left, right, preferred_element_type=F32)


def total_of(value):
    return jnp.sum(jnp.sum(value, axis=0, keepdims=True), axis=1, keepdims=True)


def iota(shape, axis):
    return lax.broadcasted_iota(jnp.int32, shape, axis)


def step_kernel(
    sizes, plan,
    near_hbm, live_ref, pos_hbm, charge_hbm, cos_hbm, diag_hbm, group_hbm, coeff_hbm, local_hbm,
    waves_ref, force_out, misc_ref,
    near_ref, pos_ref, charge_ref, cos_ref, diag_ref, group_ref, coeff_ref, local_ref, stage_ref, sect_ref,
    held_ref, field_ref, dens_ref, going_ref, back_ref, recip_ref, moment_ref, row_ref, rows_ref,
    tile_ref, gvec_tiles, band_tiles, dom_tiles, pair_ref, pairs_ref, square_ref, squares_ref,
    xg_ref, xh_ref, yg_ref, y_ref, depth_ref, zg_ref, zh_ref, scale_ref, place_ref, proj_ref,
    load_sem, local_sem, small_sem, own_sem, fsend, frecv, bsend, brecv, csend, crecv,
):
    band_size, gvec_size, dom_size = sizes
    total = band_size * gvec_size * dom_size
    x_local, extent, y_share, cap, live_total, atoms = plan
    band_id, gvec_id, dom_id = lax.axis_index("band"), lax.axis_index("gvec"), lax.axis_index("dom")
    me = (dom_id * band_size + band_id) * gvec_size + gvec_id
    band_total = band_size * dom_size
    width = len(kernel_weights) * live_total
    cells = float(extent**3)
    wave_step = np.float32(np.pi / extent)
    y_chunk = 16 if y_share % 16 == 0 else y_share
    chunks = y_share // y_chunk
    piece = 16 if x_local % 16 == 0 else x_local
    pieces = x_local // piece
    grain = 8 if x_local % 8 == 0 else x_local
    grains = x_local // grain
    first_chunks, early = max(chunks - 3, 0), max(chunks - 2, 0)
    barrier = pltpu.get_barrier_semaphore()

    def load_of(part):
        window = pl.ds(part * piece, piece)
        return pltpu.make_async_copy(coeff_hbm.at[0, window], coeff_ref.at[window], load_sem.at[part])

    smalls = [
        pltpu.make_async_copy(source, target, small_sem.at[at])
        for at, (source, target) in enumerate(
            (
                (near_hbm, near_ref), (pos_hbm, pos_ref), (charge_hbm, charge_ref),
                (cos_hbm, cos_ref), (diag_hbm, diag_ref), (group_hbm, group_ref),
            )
        )
    ]
    for copy in smalls:
        copy.start()
    for part in range(pieces):
        load_of(part).start()
    local_copy = pltpu.make_async_copy(local_hbm, local_ref, local_sem)
    local_copy.start()

    band_at = [lax.rem(band_id + shift, band_size) for shift in range(band_size)]
    gvec_at = [lax.rem(gvec_id + shift, gvec_size) for shift in range(gvec_size)]
    dom_at = [lax.rem(dom_id + shift, dom_size) for shift in range(dom_size)]

    axis_peers = (
        [(band_id, gvec_at[step], dom_id) for step in range(gvec_size)],
        [(band_at[step], gvec_id, dom_id) for step in range(band_size)],
        [(band_id, gvec_id, dom_at[step]) for step in range(dom_size)],
    )
    for peers in axis_peers:
        for peer in peers[1:]:
            pl.semaphore_signal(barrier, inc=1, device_id=peer, device_id_type=MESH)

    def exchange(kind, axis, src, dst):
        return [
            pltpu.make_async_remote_copy(
                src_ref=src, dst_ref=dst,
                send_sem=csend.at[kind, axis, step], recv_sem=crecv.at[kind, axis, step],
                device_id=axis_peers[axis][step], device_id_type=MESH,
            )
            for step in range(1, len(axis_peers[axis]))
        ]

    def start_all(copies):
        for copy in copies:
            copy.start()
        return copies

    def wait_all(copies):
        for copy in copies:
            copy.wait()

    group = piece
    smalls[3].wait()
    smalls[4].wait()

    def forward(index, carry):
        load_of(index).wait()
        for pair in range(group // 2):
            first = index * group + 2 * pair
            both = jnp.concatenate([coeff_ref[first], coeff_ref[first + 1]], axis=1)
            section = dot(both, diag_ref[0]).astype(BF16)
            result = dot(cos_ref[0], section)
            stage_ref[pl.ds(2 * pair * extent, extent)] = result[:, :extent]
            stage_ref[pl.ds((2 * pair + 1) * extent, extent)] = result[:, extent:]
        window = pl.ds(pl.multiple_of(index * group, group), group)

        def spread(outer, inner_carry):
            for inner in range(8):
                y = outer * 8 + inner
                sect_ref[y, window] = stage_ref[pl.ds(y, group, stride=extent)].astype(BF16)
            return inner_carry

        lax.fori_loop(0, extent // 8, spread, 0)
        return carry

    ahead = pieces // 2

    def gvec_peer(step):
        return (band_id, gvec_at[step], dom_id)

    def lead_copy(step, part):
        window = pl.ds(part * piece, piece)
        return pltpu.make_async_remote_copy(
            src_ref=sect_ref.at[pl.ds(gvec_at[step] * y_share, y_share), window],
            dst_ref=held_ref.at[gvec_id, :, window],
            send_sem=fsend.at[step, chunks + part], recv_sem=frecv.at[step, chunks + part],
            device_id=gvec_peer(step), device_id_type=MESH,
        )

    def forward_copy(step, chunk):
        owner = gvec_at[step]
        window = pl.ds(ahead * piece, x_local - ahead * piece)
        return pltpu.make_async_remote_copy(
            src_ref=sect_ref.at[pl.ds(owner * y_share + chunk * y_chunk, y_chunk), window],
            dst_ref=held_ref.at[gvec_id, pl.ds(chunk * y_chunk, y_chunk), window],
            send_sem=fsend.at[step, chunk], recv_sem=frecv.at[step, chunk],
            device_id=gvec_peer(step), device_id_type=MESH,
        )

    if ahead:
        forward(0, 0)

    for at in (0, 1, 2, 5):
        smalls[at].wait()

    lanes = row_ref.shape[1]
    lane = iota((1, lanes), 1)
    near_row = jnp.full((1, lanes), -1, jnp.int32)
    for quantity in range(4):
        for slot in range(cap):
            near_row = jnp.where(lane == quantity * cap + slot, near_ref[slot], near_row)
    live = live_ref[0]
    chosen = (iota((atoms, lanes), 0) == near_row).astype(F32).astype(BF16)
    values = jnp.concatenate([pos_ref[...], charge_ref[...]], axis=0)
    high = values.astype(BF16)
    rest = values - high.astype(F32)
    middle_part = rest.astype(BF16)
    low = (rest - middle_part.astype(F32)).astype(BF16)
    picked = dot(high, chosen) + dot(middle_part, chosen) + dot(low, chosen)
    row = jnp.zeros((1, lanes), F32)
    for quantity in range(3):
        part = (lane >= quantity * cap) & (lane < (quantity + 1) * cap)
        row = jnp.where(part, picked[quantity : quantity + 1], row)
    part = (lane >= 3 * cap) & (lane < 3 * cap + live) & (lane < 4 * cap)
    row = jnp.where(part, picked[3:4], row)
    row = jnp.where(lane == 4 * cap, live.astype(F32), row)
    row_ref[...] = row
    rows_ref[dom_id, band_id, gvec_id] = row

    pl.semaphore_wait(barrier, band_size + gvec_size + dom_size - 3)
    copies = start_all(exchange(0, 0, row_ref, rows_ref.at[dom_id, band_id, gvec_id]))
    if ahead:
        for step in range(1, gvec_size):
            lead_copy(step, 0).start()

    def lead(part, carry):
        forward(part, carry)
        for step in range(1, gvec_size):
            lead_copy(step, part).start()
        return carry

    lax.fori_loop(1, ahead, lead, 0)
    wait_all(copies)
    copies = start_all(exchange(0, 1, rows_ref.at[dom_id, band_id], rows_ref.at[dom_id, band_id]))
    lax.fori_loop(ahead, pieces, forward, 0)
    for chunk in range(chunks):
        for step in range(1, gvec_size):
            forward_copy(step, chunk).start()
    own_copy = pltpu.make_async_copy(
        sect_ref.at[pl.ds(gvec_id * y_share, y_share)], held_ref.at[gvec_id], own_sem.at[0]
    )
    own_copy.start()
    wait_all(copies)
    copies = start_all(exchange(0, 2, rows_ref.at[dom_id], rows_ref.at[dom_id]))

    local_copy.wait()
    x_block = 16

    def turn_local(index, carry):
        window = pl.ds(pl.multiple_of(index * x_block, x_block), x_block)
        stage_ref[pl.ds(0, x_block * y_share)] = (
            local_ref[window].astype(F32).reshape(x_block * y_share, extent)
        )

        def turn(outer, inner_carry):
            for inner in range(8):
                y = outer * 8 + inner
                field_ref[y, window] = stage_ref[pl.ds(y, x_block, stride=y_share)]
            return inner_carry

        lax.fori_loop(0, y_share // 8, turn, 0)
        return carry

    lax.fori_loop(0, extent // x_block, turn_local, 0)

    wait_all(copies)
    rows = rows_ref[...].reshape(total, row_ref.shape[1])
    count = rows[:, 4 * cap : 4 * cap + 1]
    count_wide = jnp.broadcast_to(count, (total, live_total))
    offset = jnp.dot(group_ref[...], count_wide, precision=HIGH, preferred_element_type=F32)
    order = iota((total, live_total), 1).astype(F32)
    holds = ((order >= offset) & (order < offset + count_wide)).astype(F32)
    slot_at = jnp.sum(holds * (order - offset), axis=0, keepdims=True)
    spread_rows = lax.dot_general(
        rows, holds, (((0,), (0,)), ((), ())), precision=HIGH, preferred_element_type=F32
    )
    here = (iota((cap, live_total), 0).astype(F32) == slot_at).astype(F32)
    centre = [
        jnp.sum(spread_rows[k * cap : (k + 1) * cap] * here, axis=0, keepdims=True) for k in range(4)
    ]
    mine = (iota((total, 1), 0) == me).astype(F32)
    own_offset = jnp.sum(mine * offset[:, :1], axis=0, keepdims=True)
    place_ref[...] = jnp.broadcast_to(own_offset, place_ref.shape)

    x_points = iota((extent, live_total), 0).astype(F32)
    y_points = (iota((y_share, live_total), 0) + gvec_id * y_share).astype(F32)
    for k, fraction in enumerate(sigma_fractions):
        exponent = 0.5 / (extent * fraction) ** 2
        window = slice(k * live_total, (k + 1) * live_total)
        scaled = kernel_weights[k] * centre[3]
        scale_ref[:, window] = scaled
        away = x_points - centre[0]
        value = jnp.exp(-exponent * away * away)
        xg_ref[:, window] = value
        xh_ref[:, window] = 2.0 * exponent * away * value
        away = y_points - centre[1]
        value = jnp.exp(-exponent * away * away)
        slope = 2.0 * exponent * away * value
        yg_ref[:, window] = value
        for part in range(live_total // 128):
            y_ref[0, k * live_total // 128 + part] = value[:, part * 128 : (part + 1) * 128]
            y_ref[1, k * live_total // 128 + part] = slope[:, part * 128 : (part + 1) * 128]
        away = x_points - centre[2]
        value = jnp.exp(-exponent * away * away)
        depth_ref[window] = jnp.transpose(scaled * value).astype(BF16)
        zg_ref[:, window] = value.astype(BF16)
        zh_ref[:, window] = (2.0 * exponent * away * value).astype(BF16)

    block = min(width, 512)

    field_rows = 4

    def add_field(index, carry):
        value = None
        for part in range(width // block):
            window = slice(part * block, (part + 1) * block)
            plane = jnp.concatenate(
                [
                    (xg_ref[:, window] * yg_ref[pl.ds(index * field_rows + side, 1), window]).astype(BF16)
                    for side in range(field_rows)
                ],
                axis=0,
            )
            term = dot(plane, depth_ref[window])
            value = term if value is None else value + term
        value = value.astype(BF16).astype(F32)
        for side in range(field_rows):
            field_ref[index * field_rows + side] += value[side * extent : (side + 1) * extent]
        return carry

    lax.fori_loop(0, y_share // field_rows, add_field, 0)

    def back_copy(step, chunk, part):
        owner = gvec_at[step]
        return pltpu.make_async_remote_copy(
            src_ref=going_ref.at[chunk, pl.ds(owner * x_local + part * grain, grain)],
            dst_ref=back_ref.at[gvec_id, chunk, pl.ds(part * grain, grain)],
            send_sem=bsend.at[step, chunk, part], recv_sem=brecv.at[step, chunk, part],
            device_id=gvec_peer(step), device_id_type=MESH,
        )

    def early_copy(step, chunk):
        return pltpu.make_async_remote_copy(
            src_ref=going_ref.at[chunk, pl.ds(gvec_at[step] * x_local, x_local)],
            dst_ref=back_ref.at[gvec_id, chunk],
            send_sem=bsend.at[step, chunk, 0], recv_sem=brecv.at[step, chunk, 0],
            device_id=gvec_peer(step), device_id_type=MESH,
        )

    def own_back(chunk):
        return pltpu.make_async_copy(
            going_ref.at[chunk, pl.ds(gvec_id * x_local, x_local)],
            back_ref.at[gvec_id, chunk], own_sem.at[1 + chunk],
        )

    own_copy.wait()

    q_wave = iota((extent, extent), 0).astype(F32) * wave_step
    l_wave = iota((extent, extent), 1).astype(F32) * wave_step
    plane_kinetic = 0.5 * (q_wave * q_wave + l_wave * l_wave)
    moment_ref[...] = jnp.zeros_like(moment_ref)

    def x_wave_of(a):
        return jnp.full((1, 1), gvec_id * x_local + a, jnp.int32).astype(F32) * wave_step

    def coefficients(index, carry):
        zero, one, two = 0.0, 0.0, 0.0
        for inner in range(4):
            a = index * 4 + inner
            wide = coeff_ref[a].astype(F32)
            x_wave = x_wave_of(a)
            square = wide * wide
            by_x = square * x_wave
            zero, one, two = zero + square, one + by_x, two + by_x * x_wave
            recip_ref[a] = step_size / (1.0 + 0.5 * x_wave * x_wave + plane_kinetic)
        moment_ref[0] += zero
        moment_ref[1] += one
        moment_ref[2] += two
        return carry

    lax.fori_loop(0, x_local // 4, coefficients, 0)
    group_id = band_id * dom_size + dom_id
    shifted = jnp.full((1, 1), group_id, jnp.int32).astype(F32) - 0.5 * band_total
    weight = 2.0 / (1.0 + jnp.exp(shifted / (0.125 * band_total)))
    terms = (
        moment_ref[2],
        moment_ref[0] * q_wave * q_wave,
        moment_ref[0] * l_wave * l_wave,
        moment_ref[1] * q_wave,
        moment_ref[1] * l_wave,
        moment_ref[0] * q_wave * l_wave,
    )
    terms = [total_of(term) for term in terms]
    stress = [weight * term / cells for term in terms]
    norm = total_of(moment_ref[0])

    for step in range(1, gvec_size):
        for part in range(ahead):
            lead_copy(step, part).wait_recv()

    def middle(chunk, inner):
        for step in range(1, gvec_size):
            forward_copy(step, chunk).wait_recv()
        for pair in range(y_chunk // 2):
            first = chunk * y_chunk + 2 * pair
            both = jnp.concatenate(
                [
                    jnp.concatenate([held_ref[source, first + side] for source in range(gvec_size)], axis=0)
                    for side in range(2)
                ],
                axis=1,
            )
            wide = dot(cos_ref[0], both).astype(BF16).astype(F32)
            square = (wide * wide).astype(BF16)
            dens_ref[first] = square[:, :extent]
            dens_ref[first + 1] = square[:, extent:]
            fields = jnp.concatenate([field_ref[first], field_ref[first + 1]], axis=1)
            applied = (fields * wide).astype(BF16)
            result = dot(cos_ref[1], applied)
            stage_ref[pl.ds(2 * pair * extent, extent)] = result[:, :extent]
            stage_ref[pl.ds((2 * pair + 1) * extent, extent)] = result[:, extent:]
            inner = inner + jnp.sum((applied.astype(F32) * wide).reshape(-1, 8, 2 * extent), axis=0)

        def spread(outer, inner_carry):
            for side in range(8):
                a = outer * 8 + side
                going_ref[chunk, a] = stage_ref[pl.ds(a, y_chunk, stride=extent)].astype(BF16)
            return inner_carry

        lax.fori_loop(0, extent // 8, spread, 0)
        own_back(chunk).start()
        return inner

    def middle_early(chunk, inner):
        inner = middle(chunk, inner)
        for step in range(1, gvec_size):
            early_copy(step, chunk).start()
        return inner

    inner = lax.fori_loop(0, first_chunks, middle_early, jnp.zeros((8, 2 * extent), F32))
    inner = lax.fori_loop(first_chunks, chunks, middle, inner)

    inner = total_of(inner) + 0.5 * (terms[0] + terms[1] + terms[2])
    pair_ref[0:1] = jnp.broadcast_to(norm, (1, 128))
    pair_ref[1:2] = jnp.broadcast_to(inner, (1, 128))
    pairs_ref[gvec_id] = pair_ref[...]
    pair_copies = start_all(exchange(2, 0, pair_ref, pairs_ref.at[gvec_id]))
    for chunk in range(first_chunks, early):
        for step in range(1, gvec_size):
            early_copy(step, chunk).start()

    x_part = 32

    def project(index, carry):
        at = pl.ds(pl.multiple_of(index * 128, 128), 128)
        tables = jnp.concatenate([zg_ref[:, at], zh_ref[:, at]], axis=1)

        def over_x(x_at, sums):
            x_window = pl.ds(pl.multiple_of(x_at * x_part, x_part), x_part)
            result = dot(dens_ref[:, x_window].reshape(y_share * x_part, extent), tables)
            along, slope, deep = 0.0, 0.0, 0.0
            for y in range(y_share):
                rows_at = slice(y * x_part, (y + 1) * x_part)
                value, derivative = y_ref[0, index, pl.ds(y, 1)], y_ref[1, index, pl.ds(y, 1)]
                along = along + result[rows_at, :128] * value
                slope = slope + result[rows_at, :128] * derivative
                deep = deep + result[rows_at, 128:] * value
            value, derivative = xg_ref[x_window, at], xh_ref[x_window, at]
            terms = (derivative * along, value * slope, value * deep, value * along)
            return tuple(
                old + jnp.sum(term.reshape(-1, 8, 128), axis=0) for old, term in zip(sums, terms)
            )

        start = tuple(jnp.zeros((8, 128), F32) for _ in range(4))
        sums = lax.fori_loop(0, extent // x_part, over_x, start)
        for at_sum in range(4):
            total_row = jnp.sum(sums[at_sum], axis=0, keepdims=True)
            proj_ref[at_sum : at_sum + 1, at] = total_row * scale_ref[:, at]
        return carry

    lax.fori_loop(0, width // 128, project, 0)
    folded = jnp.zeros((4, live_total), F32)
    for k in range(len(kernel_weights)):
        folded = folded + proj_ref[:, k * live_total : (k + 1) * live_total]
    tile_ref[0:3] = (-force_unit * weight) * folded[0:3]
    embedding = weight * jnp.sum(folded[3:4], axis=1, keepdims=True) / cells
    line = jnp.zeros((1, live_total), F32)
    tile_lane = iota((1, live_total), 1)
    wait_all(pair_copies)
    both = sum(pairs_ref[source] for source in range(gvec_size))
    norm, inner = both[0:1], both[1:2]
    energy = inner / norm
    misc_ref[0:1] = energy
    band_energy = weight * energy[:, 0:1] / float(gvec_size * band_total)
    for at, value in enumerate(stress + [embedding, band_energy]):
        line = jnp.where(tile_lane == at, value, line)
    tile_ref[3:4] = line

    def tile_stage(axis, slots, at):
        slots[at] = tile_ref[...]
        return start_all(exchange(1, axis, tile_ref, slots.at[at]))

    def tile_sum(copies, slots):
        wait_all(copies)
        value = slots[0]
        for source in range(1, slots.shape[0]):
            value = value + slots[source]
        tile_ref[...] = value

    copies = tile_stage(0, gvec_tiles, gvec_id)

    def send_late(part, carry):
        for chunk in range(early, chunks):
            for step in range(1, gvec_size):
                back_copy(step, chunk, part).start()
        return carry

    lax.fori_loop(0, grains, send_late, 0)

    for chunk in range(chunks):
        own_back(chunk).wait()
    for chunk in range(early):
        for step in range(1, gvec_size):
            early_copy(step, chunk).wait_recv()

    def image_of(part, square):
        for chunk in range(early, chunks):
            for step in range(1, gvec_size):
                back_copy(step, chunk, part).wait_recv()
        for pair in range(grain // 2):
            first = part * grain + 2 * pair
            both = jnp.concatenate(
                [
                    jnp.concatenate(
                        [
                            back_ref[source, chunk, first + side]
                            for source in range(gvec_size)
                            for chunk in range(chunks)
                        ],
                        axis=0,
                    )
                    for side in range(2)
                ],
                axis=1,
            )
            section = dot(cos_ref[1], both).astype(BF16)
            waves = dot(section, diag_ref[1])
            for side in range(2):
                a = first + side
                wide = coeff_ref[a].astype(F32)
                x_wave = x_wave_of(a)
                image = (0.5 * x_wave * x_wave + plane_kinetic) * wide
                image = image + waves[:, side * extent : (side + 1) * extent]
                residual = image - energy * wide
                square = square + jnp.sum((residual * residual).reshape(-1, 8, extent), axis=0)
                waves_ref[0, a] = (wide - residual * recip_ref[a]).astype(BF16)
        return square

    cuts = [(grains - 1) * at // 3 for at in range(4)]
    square = lax.fori_loop(cuts[0], cuts[1], image_of, jnp.zeros((8, extent), F32))
    tile_sum(copies, gvec_tiles)
    copies = tile_stage(1, band_tiles, band_id)
    square = lax.fori_loop(cuts[1], cuts[2], image_of, square)
    tile_sum(copies, band_tiles)
    copies = tile_stage(2, dom_tiles, dom_id)
    square = lax.fori_loop(cuts[2], cuts[3], image_of, square)
    tile_sum(copies, dom_tiles)

    summed = tile_ref[...]
    slot_lanes = (iota((live_total, 128), 0).astype(F32) - place_ref[0:1, 0:1]) == iota(
        (live_total, 128), 1
    ).astype(F32)
    slot_lanes = slot_lanes & (iota((live_total, 128), 1) < live)
    slot_force = jnp.dot(summed, slot_lanes.astype(F32), precision=HIGH, preferred_element_type=F32)
    near_column = jnp.full((128, 1), -1, jnp.int32)
    for slot in range(cap):
        near_column = jnp.where(iota((128, 1), 0) == slot, near_ref[slot], near_column)
    at_atom = (iota((128, atoms), 1) == near_column).astype(F32)
    atom_force = jnp.dot(slot_force, at_atom, precision=HIGH, preferred_element_type=F32)
    force_out[...] = atom_force[0:3]
    misc_ref[2:3] = summed[3:4, 0:128]
    misc_ref[3:8] = jnp.zeros((5, 128), F32)

    square = image_of(grains - 1, square)
    square_ref[...] = jnp.broadcast_to(total_of(square), (1, 128))
    squares_ref[gvec_id] = square_ref[...]
    wait_all(start_all(exchange(3, 0, square_ref, squares_ref.at[gvec_id])))
    square = sum(squares_ref[source] for source in range(gvec_size))
    misc_ref[1:2] = square / norm

    for step in range(1, gvec_size):
        for part in range(ahead):
            lead_copy(step, part).wait_send()
        for chunk in range(chunks):
            forward_copy(step, chunk).wait_send()
        for chunk in range(early):
            early_copy(step, chunk).wait_send()
        for chunk in range(early, chunks):
            for part in range(grains):
                back_copy(step, chunk, part).wait_send()


def finish_kernel(
    parts, waves_ref, force_ref, misc_ref,
    waves_hbm, force_hbm, energy_hbm, ratio_hbm, total_hbm, energy_ref, ratio_ref, total_ref, sems,
):
    size = waves_ref.shape[1] // parts
    pairs = [
        (waves_ref.at[:, pl.ds(part * size, size)], waves_hbm.at[:, pl.ds(part * size, size)])
        for part in range(parts)
    ]
    pairs += [
        (force_ref, force_hbm), (energy_ref, energy_hbm), (ratio_ref, ratio_hbm), (total_ref, total_hbm)
    ]
    copies = [
        pltpu.make_async_copy(source, target, sems.at[at]) for at, (source, target) in enumerate(pairs)
    ]
    for copy in copies[: parts + 1]:
        copy.start()
    energy_ref[...] = misc_ref[0:1, 0:1]
    ratio_ref[...] = misc_ref[1:2, 0:1]
    total_ref[...] = misc_ref[2:3, 0:8]
    for copy in copies[parts + 1 :]:
        copy.start()
    for copy in copies:
        copy.wait()


def per_device(sizes, coeffs, v_local, atom_pos, atom_charge, near_list, live_count):
    band_size, gvec_size, dom_size = sizes
    total = sizes[0] * sizes[1] * sizes[2]
    local_bands, x_local, extent, _ = coeffs.shape
    assert local_bands == 1
    y_share = v_local.shape[1]
    cap = near_list.shape[0]
    atoms = atom_pos.shape[1]
    live_total = total * cap // 4
    width = len(kernel_weights) * live_total
    y_chunk = 16 if y_share % 16 == 0 else y_share
    chunks = y_share // y_chunk
    piece = 16 if x_local % 16 == 0 else x_local
    pieces = x_local // piece
    grains = x_local // (8 if x_local % 8 == 0 else x_local)
    lanes = -(-(4 * cap + 1) // 128) * 128
    pair, diagonal = constant_tables(extent)
    groups = np.tril(np.ones((total, total), np.float32), -1)
    vmem = pl.BlockSpec(memory_space=pltpu.VMEM)
    smem = pl.BlockSpec(memory_space=pltpu.SMEM)
    hbm = pl.BlockSpec(memory_space=pltpu.HBM)
    plan = (x_local, extent, y_share, cap, live_total, atoms)
    deep = max(piece, y_chunk, 16)
    dma = pltpu.SemaphoreType.DMA
    operands = [
        pltpu.with_memory_space_constraint(operand, pltpu.HBM)
        for operand in (
            near_list, atom_pos, atom_charge.reshape(1, atoms), jnp.asarray(pair),
            jnp.asarray(diagonal), jnp.asarray(groups), coeffs, v_local,
        )
    ]
    scalar = jax.ShapeDtypeStruct((1, 1), F32)
    outs = (
        jax.ShapeDtypeStruct(coeffs.shape, BF16), jax.ShapeDtypeStruct((3, atoms), F32),
        scalar, scalar, jax.ShapeDtypeStruct((1, 8), F32),
    )
    results = pl.pallas_call(
        functools.partial(step_kernel, sizes, plan),
        out_shape=(outs[0], outs[1], jax.ShapeDtypeStruct((8, 128), F32)),
        in_specs=[hbm, smem] + [hbm] * 7,
        out_specs=(vmem,) * 3,
        scratch_shapes=[
            pltpu.SMEM(near_list.shape, jnp.int32),
            pltpu.VMEM(atom_pos.shape, F32),
            pltpu.VMEM((1, atoms), F32),
            pltpu.VMEM(pair.shape, BF16),
            pltpu.VMEM(diagonal.shape, BF16),
            pltpu.VMEM(groups.shape, F32),
            pltpu.VMEM((x_local, extent, extent), BF16),
            pltpu.VMEM(v_local.shape, BF16),
            pltpu.VMEM((deep * extent, extent), F32),
            pltpu.VMEM((extent, x_local, extent), BF16),
            pltpu.VMEM((gvec_size, y_share, x_local, extent), BF16),
            pltpu.VMEM((y_share, extent, extent), F32),
            pltpu.VMEM((y_share, extent, extent), BF16),
            pltpu.VMEM((chunks, extent, y_chunk, extent), BF16),
            pltpu.VMEM((gvec_size, chunks, x_local, y_chunk, extent), BF16),
            pltpu.VMEM((x_local, extent, extent), F32),
            pltpu.VMEM((3, extent, extent), F32),
            pltpu.VMEM((1, lanes), F32),
            pltpu.VMEM((dom_size, band_size, gvec_size, 1, lanes), F32),
            pltpu.VMEM((4, live_total), F32),
            pltpu.VMEM((gvec_size, 4, live_total), F32),
            pltpu.VMEM((band_size, 4, live_total), F32),
            pltpu.VMEM((dom_size, 4, live_total), F32),
            pltpu.VMEM((2, 128), F32),
            pltpu.VMEM((gvec_size, 2, 128), F32),
            pltpu.VMEM((1, 128), F32),
            pltpu.VMEM((gvec_size, 1, 128), F32),
            pltpu.VMEM((extent, width), F32),
            pltpu.VMEM((extent, width), F32),
            pltpu.VMEM((y_share, width), F32),
            pltpu.VMEM((2, width // 128, y_share, 128), F32),
            pltpu.VMEM((width, extent), BF16),
            pltpu.VMEM((extent, width), BF16),
            pltpu.VMEM((extent, width), BF16),
            pltpu.VMEM((1, width), F32),
            pltpu.VMEM((8, 128), F32),
            pltpu.VMEM((4, width), F32),
            dma((pieces,)),
            dma,
            dma((6,)),
            dma((1 + chunks,)),
            dma((gvec_size, chunks + pieces // 2)),
            dma((gvec_size, chunks + pieces // 2)),
            dma((gvec_size, chunks, grains)),
            dma((gvec_size, chunks, grains)),
            dma((4, 3, max(sizes))),
            dma((4, 3, max(sizes))),
        ],
        compiler_params=pltpu.CompilerParams(
            collective_id=0, has_side_effects=True, vmem_limit_bytes=36 * 1024 * 1024
        ),
        name="step",
    )(operands[0], live_count, *operands[1:])
    parts = 4 if x_local % 4 == 0 else 1
    waves_new, atom_force, energy, ratio, totals = pl.pallas_call(
        functools.partial(finish_kernel, parts),
        out_shape=outs,
        in_specs=[vmem] * 3,
        out_specs=(hbm,) * 5,
        scratch_shapes=[
            pltpu.VMEM((1, 1), F32), pltpu.VMEM((1, 1), F32), pltpu.VMEM((1, 8), F32), dma((parts + 4,)),
        ],
        compiler_params=pltpu.CompilerParams(vmem_limit_bytes=8 * 1024 * 1024),
        name="finish",
    )(*results)
    return (waves_new, energy.reshape(1), ratio.reshape(1), atom_force, totals.reshape(8))


def solution(mesh):
    sizes = (mesh.shape["band"], mesh.shape["gvec"], mesh.shape["dom"])
    return jax.shard_map(
        functools.partial(per_device, sizes),
        mesh=mesh,
        in_specs=(
            P(("band", "dom"), "gvec", None, None),
            P(None, "gvec", None),
            P(None, ("band", "gvec", "dom")),
            P(("band", "gvec", "dom")),
            P(("band", "gvec", "dom")),
            P(("band", "gvec", "dom")),
        ),
        out_specs=(
            P(("band", "dom"), "gvec", None, None),
            P(("band", "dom")),
            P(("band", "dom")),
            P(None, ("band", "gvec", "dom")),
            P(),
        ),
        check_vma=False,
    )
```
